32 devices in a mesh: feat: 4 (over z), tok: 8 (over y, x, core).
Axes of the slice: x: 2, y: 2, z: 4, core: 2. Of those that a mesh axis runs over, the one named last changes fastest.
Arguments:
- tokens: bfloat16 [512, 8192], P('tok'), may hold values from -6 to 6
- dec_bias: bfloat16 [8192], replicated, may hold values from -3 to 3
- enc_weight: bfloat16 [8192, 8192], P('tok', 'feat'), may hold values from -0.0625 to 0.0625
- enc_bias: bfloat16 [8192], P('feat'), may hold values from -3 to 3
- dec_weight: bfloat16 [8192, 8192], P('feat', 'tok'), may hold values from -0.25 to 0.25
- block_ids: int32 [8, 4, 4], P(None, 'feat'), may hold values from 0 to 31, as said below
- block_counts: int32 [8, 4], P(None, 'feat'), may hold values from 1 to 4, as said below
Outputs:
- code_values: bfloat16 [512, 1024], P('tok', 'feat')
- rebuilt: bfloat16 [512, 8192], P('tok', 'feat')
The draws below stay inside these ranges and needn't reach their ends.
Inputs may be any that keep to these rules, and one draw needn't show every extreme that they name: `block_ids`: the 4 entries of one list are distinct; they number the owner's 32 blocks. `block_counts`: for every owner some tile has all 4 slots active.
All inputs are finite; a program needn't handle non-finite values.
Results may differ from the reference program's by a relative error of at most 0.029.
Values may be sent and summed in bfloat16 or wider, within the bound.
No kernel may reach another device: no remote copies, remote signals or barrier semaphores. Data moves between devices by JAX's collectives and lax.ppermute only.
A program may use at most 64 MiB of HBM per device.

```python
import jax
import jax.numpy as jnp
from jax import lax

D = 8192
BLOCK = 64
BLK_DEV = 32
SLOTS = 4
TOK_DEV = 64
TILES = 8
OWNERS = 4
TOKENS = 512
FEATS = 8192
WSLICE = 1024
CODES = 1024


def draw_block_ids(key, part):
    lists = jax.random.split(jax.random.fold_in(key, 11), TILES * OWNERS)
    picks = jax.vmap(lambda single: jax.random.permutation(single, BLK_DEV)[:SLOTS])(lists)
    return picks.reshape(TILES, OWNERS, SLOTS).astype(jnp.int32)


def draw_block_counts(key, part):
    base = jax.random.randint(jax.random.fold_in(key, 21), (TILES, OWNERS), 1, SLOTS + 1)
    full_tile = jax.random.randint(jax.random.fold_in(key, 22), (OWNERS,), 0, TILES)
    tile_index = jnp.arange(TILES, dtype=jnp.int32)[:, None]
    return jnp.where(tile_index == full_tile[None, :], SLOTS, base).astype(jnp.int32)


def spiked(array, rng, source, target, blocks, factor):
    owner, partner = [(jnp.arange(array.shape[axis_at]) // (array.shape[axis_at] // blocks)).reshape([-1 if axis == axis_at else 1 for axis in range(array.ndim)]) for axis_at in (source, target)]
    chosen = jax.random.permutation(rng, blocks)[partner]
    strong = (owner == chosen) | (owner == (partner + blocks // 2) % blocks)
    return jnp.where(strong, factor * array, array)


def levels(rng, extent, pieces, smallest, top_value):
    def one(position, parts):
        draws = jax.random.uniform(jax.random.fold_in(jax.random.fold_in(rng, 6), position), (parts,), jnp.float32, smallest / len(pieces), top_value / len(pieces))
        return jnp.repeat(jnp.exp(draws), extent[position] // parts).reshape((-1,) + (1,) * (len(extent) - position - 1))

    level = one(*pieces[0])
    for cut in pieces[1:]:
        level = level * one(*cut)
    return level


def bell_draw(key, dims, scale, most, cuts=(), kind=jnp.bfloat16):
    array = scale * jax.random.normal(key, dims, jnp.float32)
    if cuts:
        array = array * levels(key, dims, cuts, -0.22, 0.18)
    return jnp.clip(array, -most, most).astype(kind)


def bell_draw_with(own_key, shape, deviation, bound, pieces, heavy, kind=jnp.bfloat16):
    drawn = deviation * jax.random.normal(own_key, shape, jnp.float32)
    if pieces:
        drawn = drawn * levels(own_key, shape, pieces, -0.22, 0.18)
    return jnp.clip(spiked(drawn, jax.random.fold_in(own_key, 3), *heavy), -bound, bound).astype(kind)


def setup_inputs(seed: int = 0) -> dict:
    key_list = jax.random.split(jax.random.key(seed), 8)
    return {
        "tokens": bell_draw(key_list[0], (TOKENS, D), 1.0, 6.0, ((0, 8),)),
        "dec_bias": bell_draw(key_list[1], (D,), 0.5, 3.0),
        "enc_weight": bell_draw(key_list[2], (D, FEATS), D ** -0.5, 0.0625, ((0, 8), (1, 4))),
        "enc_bias": bell_draw(key_list[3], (FEATS,), 0.5, 3.0, ((0, 4),)),
        "dec_weight": bell_draw_with(key_list[4], (FEATS, D), CODES ** -0.5, 0.25, ((0, 4), (1, 8)), (0, 1, 8, 2.0)),
        "block_ids": draw_block_ids(jax.random.fold_in(key_list[7], 71), 0),
        "block_counts": draw_block_counts(jax.random.fold_in(key_list[7], 71), 0),
    }


def settle(values):
    return lax.optimization_barrier(values.astype(jnp.bfloat16)).astype(jnp.float32)


def reference(tokens, dec_bias, enc_weight, enc_bias, dec_weight, block_ids, block_counts):
    centered = (tokens.astype(jnp.float32) - dec_bias.astype(jnp.float32)).astype(jnp.bfloat16)
    tile_rows = centered.reshape(TILES, TOK_DEV, D)
    owner_base = jnp.arange(OWNERS, dtype=jnp.int32)[:, None] * BLK_DEV
    nblocks = FEATS // BLOCK
    enc_blocks = enc_weight.reshape(TILES, WSLICE, nblocks, BLOCK)
    enc_bias_blocks = enc_bias.reshape(nblocks, BLOCK)
    dec_blocks = dec_weight.reshape(nblocks, BLOCK, D)
    slot_index = jnp.arange(SLOTS, dtype=jnp.int32)

    def one_tile(inputs):
        rows, listed, counted = inputs
        global_ids = (owner_base + listed.astype(jnp.int32)).reshape(-1)
        enc_cols = jnp.take(enc_blocks, global_ids, axis=2).reshape(TILES, WSLICE, CODES)
        slices = rows.reshape(TOK_DEV, TILES, WSLICE)
        part = jnp.einsum('rui,uic->urc', slices.astype(jnp.float32), enc_cols.astype(jnp.float32))
        pre = jnp.sum(settle(part), axis=0)
        pre = pre + jnp.take(enc_bias_blocks, global_ids, axis=0).reshape(CODES).astype(jnp.float32)
        live_mask = slot_index[None, :] < counted[:, None]
        live_mask = jnp.repeat(live_mask.reshape(OWNERS * SLOTS), BLOCK)
        codes_tile = jnp.where(live_mask[None, :], jnp.maximum(pre, 0.0), 0.0).astype(jnp.bfloat16)
        dec_rows = jnp.take(dec_blocks, global_ids, axis=0).reshape(OWNERS, SLOTS * BLOCK, D)
        per_owner = jnp.einsum('rfc,fcd->frd', codes_tile.reshape(TOK_DEV, OWNERS, SLOTS * BLOCK).astype(jnp.float32), dec_rows.astype(jnp.float32))
        total = jnp.sum(settle(per_owner), axis=0) + dec_bias.astype(jnp.float32)[None, :]
        return codes_tile, total.astype(jnp.bfloat16)

    codes_all, rebuilt_all = lax.map(one_tile, (tile_rows, block_ids, block_counts))
    return codes_all.reshape(TOKENS, CODES), rebuilt_all.reshape(TOKENS, D)
```

```python
import functools

import jax
import jax.numpy as jnp
from jax import lax
from jax.experimental import pallas as pl
from jax.experimental.pallas import tpu as pltpu
from jax.sharding import PartitionSpec as P

BLOCK = 64
SLOTS = 4
LANES = 128
ACTIVE = SLOTS * BLOCK
VMEM = pltpu.VMEM
SMEM = pltpu.SMEM
BF16 = jnp.bfloat16
F32 = jnp.float32


def spec(space):
    return pl.BlockSpec(memory_space=space)


def params(mib):
    return pltpu.CompilerParams(vmem_limit_bytes=mib << 20)


def cost(flops, nbytes):
    return pl.CostEstimate(flops=flops, bytes_accessed=nbytes, transcendentals=0)


def place():
    tok = lax.axis_index("tok")
    return lax.axis_index("feat"), tok >> 1, tok & 1


def center_kernel(groups, wslice, tok_ref, bias_ref, *outs):
    _, c, k = place()
    for p in range(groups):
        for half in range(2):
            u = ((c ^ p) << 1) + (k ^ half)
            cols = pl.ds(pl.multiple_of(u * wslice, wslice), wslice)
            rows = tok_ref[:, cols].astype(F32) - bias_ref[pl.ds(u, 1), :]
            outs[p][half] = rows.astype(BF16)


def pick_pair(first, second, odd_first, odd_second):
    low = lax.broadcasted_iota(jnp.int32, first.shape, 1) < BLOCK
    a = jnp.where(odd_first, pltpu.roll(first, BLOCK, 1), first)
    b = jnp.where(odd_second, second, pltpu.roll(second, BLOCK, 1))
    return jnp.where(low, a, b)


def gather_kernel(groups, ids_ref, w_ref, out_ref):
    _, c, k = place()
    for p in range(groups):
        tile = ((c ^ p) << 1) + k
        for pair in range(SLOTS // 2):
            windows = []
            odds = []
            for slot in (2 * pair, 2 * pair + 1):
                block = ids_ref[tile, slot]
                start = pl.multiple_of((block >> 1) * LANES, LANES)
                windows.append(w_ref[:, pl.ds(start, LANES)])
                odds.append((block & 1) == 1)
            picked = pick_pair(windows[0].astype(F32), windows[1].astype(F32), *odds)
            out_ref[p, :, pair * LANES : (pair + 1) * LANES] = picked.astype(BF16)


def encode_kernel(groups, *refs):
    pieces, (own_ref, oth_ref, out_ref) = refs[:groups], refs[groups:]
    step = pl.program_id(0)
    for p in range(groups):

        @pl.when(step == p)
        def _(p=p):
            acc = jnp.dot(pieces[p][0], own_ref[0], preferred_element_type=F32)
            acc += jnp.dot(pieces[p][1], oth_ref[0], preferred_element_type=F32)
            out_ref[0] = acc.astype(BF16)


def decode_kernel(groups, *refs):
    ids_ref, counts_ref, bias_ref = refs[:3]
    parts = refs[3 : 3 + groups]
    own_ref, oth_ref = refs[3 + groups : 5 + groups]
    code_ref = refs[5 + groups]
    outs = refs[6 + groups : 6 + 2 * groups]
    codes, own_rows, oth_rows, sems = refs[6 + 2 * groups :]
    f, c, k = place()
    copies = []
    for s in range(groups):
        tile = ((c ^ f ^ s) << 1) + k
        for slot in range(SLOTS):
            rows = pl.ds(pl.multiple_of(ids_ref[tile, slot] * BLOCK, BLOCK), BLOCK)
            into = pl.ds(slot * BLOCK, BLOCK)
            for which, (src, dst) in enumerate(((own_ref, own_rows), (oth_ref, oth_rows))):
                copy = pltpu.make_async_copy(
                    src.at[rows, :], dst.at[s, into, :], sems.at[s, slot, which]
                )
                copy.start()
                copies.append(copy)
    lane = lax.broadcasted_iota(jnp.int32, (1, LANES), 1)
    for p in range(groups):
        tile = ((c ^ p) << 1) + k
        count = counts_ref[tile]
        for pair in range(SLOTS // 2):
            cols = slice(pair * LANES, (pair + 1) * LANES)
            pre = parts[0][p, :, cols].astype(F32)
            for q in range(1, groups):
                pre += parts[q][p ^ q, :, cols].astype(F32)
            bias = []
            odds = []
            for slot in (2 * pair, 2 * pair + 1):
                block = ids_ref[tile, slot]
                bias.append(bias_ref[pl.ds(block >> 1, 1), :])
                odds.append((block & 1) == 1)
            row = pick_pair(bias[0], bias[1], *odds)
            live = (lane >= BLOCK).astype(jnp.int32) + 2 * pair < count
            value = jnp.where(live, jnp.maximum(pre + row, 0.0), 0.0).astype(BF16)
            codes[p, :, cols] = value
    code_ref[...] = codes[0]
    per_step = 2 * SLOTS
    for s in range(groups):
        for copy in copies[s * per_step : (s + 1) * per_step]:
            copy.wait()
        code = codes[f ^ s]
        own = jnp.dot(code, own_rows[s], preferred_element_type=F32)
        outs[s][k] = own.astype(BF16)
        oth = jnp.dot(code, oth_rows[s], preferred_element_type=F32)
        outs[s][1 - k] = oth.astype(BF16)


def finish_kernel(groups, *refs):
    arrived, (bias_ref, out_ref) = refs[:groups], refs[groups:]
    f, _, _ = place()
    wslice = arrived[0].shape[2]
    for half in range(2):
        total = arrived[0][half].astype(F32)
        for ref in arrived[1:]:
            total += ref[half].astype(F32)
        total += bias_ref[pl.ds(2 * f + half, 1), :]
        out_ref[:, half * wslice : (half + 1) * wslice] = total.astype(BF16)


def on_device(tokens, dec_bias, enc_weight, enc_bias, dec_weight, block_ids, block_counts):
    tile_count = lax.axis_size("tok")
    groups = lax.axis_size("feat")
    tok_rows, width = tokens.shape
    wslice = width // tile_count
    feats = enc_weight.shape[1]
    ids = block_ids[:, 0, :]
    counts = block_counts[:, 0]
    bias_rows = dec_bias.astype(F32).reshape(tile_count, wslice)
    enc_bias_rows = enc_bias.astype(F32).reshape(feats // LANES, LANES)

    def swap(value, p):
        pairs = [(i, i ^ (2 * p)) for i in range(tile_count)]
        return lax.ppermute(value, "tok", pairs)

    cores = [(i, i ^ 1) for i in range(tile_count)]
    enc_other = lax.ppermute(enc_weight, "tok", cores)
    dec_other = lax.ppermute(dec_weight, "tok", cores)

    piece = jax.ShapeDtypeStruct((2, tok_rows, wslice), BF16)
    sent = pl.pallas_call(
        functools.partial(center_kernel, groups, wslice),
        out_shape=[piece] * groups,
        in_specs=[spec(VMEM)] * 2,
        out_specs=[spec(VMEM)] * groups,
        compiler_params=params(16),
        cost_estimate=cost(width * tok_rows, 4 * width * tok_rows),
        name="center",
    )(tokens, bias_rows)
    pieces = [sent[0]] + [swap(sent[p], p) for p in range(1, groups)]

    chunk = min(wslice, 256)

    def gather(weight):
        return pl.pallas_call(
            functools.partial(gather_kernel, groups),
            out_shape=jax.ShapeDtypeStruct((groups, wslice, ACTIVE), BF16),
            grid=(wslice // chunk,),
            in_specs=[spec(SMEM), pl.BlockSpec((chunk, feats), lambda i: (i, 0))],
            out_specs=pl.BlockSpec((groups, chunk, ACTIVE), lambda i: (0, i, 0)),
            compiler_params=params(32),
            cost_estimate=cost(0, 2 * wslice * (feats + groups * ACTIVE)),
            name="pick_columns",
        )(ids, weight)

    own_cols = gather(enc_weight)
    oth_cols = gather(enc_other)
    col_spec = pl.BlockSpec((1, wslice, ACTIVE), lambda i: (i, 0, 0))
    part = pl.pallas_call(
        functools.partial(encode_kernel, groups),
        out_shape=jax.ShapeDtypeStruct((groups, tok_rows, ACTIVE), BF16),
        grid=(groups,),
        in_specs=[spec(VMEM)] * groups + [col_spec] * 2,
        out_specs=pl.BlockSpec((1, tok_rows, ACTIVE), lambda i: (i, 0, 0)),
        compiler_params=params(32),
        cost_estimate=cost(
            4 * groups * tok_rows * wslice * ACTIVE, 4 * groups * wslice * ACTIVE
        ),
        name="encode",
    )(*pieces, own_cols, oth_cols)
    parts = [part] + [swap(part, p) for p in range(1, groups)]

    decoded = pl.pallas_call(
        functools.partial(decode_kernel, groups),
        out_shape=[jax.ShapeDtypeStruct((tok_rows, ACTIVE), BF16)] + [piece] * groups,
        in_specs=[spec(SMEM)] * 2 + [spec(VMEM)] * (1 + groups) + [spec(pl.ANY)] * 2,
        out_specs=[spec(VMEM)] * (1 + groups),
        scratch_shapes=[
            VMEM((groups, tok_rows, ACTIVE), BF16),
            VMEM((groups, ACTIVE, wslice), BF16),
            VMEM((groups, ACTIVE, wslice), BF16),
            pltpu.SemaphoreType.DMA((groups, SLOTS, 2)),
        ],
        compiler_params=params(40),
        cost_estimate=cost(
            4 * groups * tok_rows * wslice * ACTIVE, 4 * groups * wslice * ACTIVE
        ),
        name="decode",
    )(ids, counts, enc_bias_rows, *parts, dec_weight, dec_other)
    code_values, outgoing = decoded[0], decoded[1:]

    arrived = []
    for s in range(groups):
        plane = []
        line = []
        for f in range(groups):
            for i in range(tile_count):
                here = f * tile_count + i
                plane.append((here, f * tile_count + (i ^ (2 * (f ^ s)))))
                line.append((here, ((i >> 1) ^ f ^ s) * tile_count + i))
        moved = lax.ppermute(outgoing[s], ("feat", "tok"), plane)
        arrived.append(lax.ppermute(moved, ("feat", "tok"), line))

    rebuilt = pl.pallas_call(
        functools.partial(finish_kernel, groups),
        out_shape=jax.ShapeDtypeStruct((tok_rows, 2 * wslice), BF16),
        in_specs=[spec(VMEM)] * (groups + 1),
        out_specs=spec(VMEM),
        compiler_params=params(16),
        cost_estimate=cost(0, 2 * (groups + 1) * 2 * tok_rows * wslice),
        name="finish",
    )(*arrived, bias_rows)
    return (code_values, rebuilt)


def solution(mesh):
    in_specs = (
        P("tok", None),
        P(),
        P("tok", "feat"),
        P("feat"),
        P("feat", "tok"),
        P(None, "feat", None),
        P(None, "feat"),
    )
    out_specs = (P("tok", "feat"), P("tok", "feat"))
    return jax.shard_map(
        on_device, mesh=mesh, in_specs=in_specs, out_specs=out_specs, check_vma=False
    )
```

```python
import functools

import jax
import jax.numpy as jnp
from jax import lax
from jax.experimental import pallas as pl
from jax.experimental.pallas import tpu as pltpu
from jax.sharding import PartitionSpec as P

BLOCK = 64
SLOTS = 4
LANES = 128
ACTIVE = SLOTS * BLOCK
CHUNKS = 2
VMEM = pltpu.VMEM
SMEM = pltpu.SMEM
BF16 = jnp.bfloat16
F32 = jnp.float32


def spec(space):
    return pl.BlockSpec(memory_space=space)


def params(mib):
    return pltpu.CompilerParams(vmem_limit_bytes=mib << 20)


def cost(flops, nbytes):
    return pl.CostEstimate(flops=flops, bytes_accessed=nbytes, transcendentals=0)


def place():
    tok = lax.axis_index("tok")
    return lax.axis_index("feat"), tok >> 1, tok & 1


def center_kernel(groups, wslice, chunks, tok_ref, bias_ref, *outs):
    _, c, k = place()
    rows = tok_ref.shape[0] // chunks
    for h in range(chunks):
        for p in range(groups):
            for half in range(2):
                u = ((c ^ p) << 1) + (k ^ half)
                cols = pl.ds(pl.multiple_of(u * wslice, wslice), wslice)
                value = tok_ref[h * rows : (h + 1) * rows, cols].astype(F32)
                value -= bias_ref[pl.ds(u, 1), :]
                outs[h * groups + p][half] = value.astype(BF16)


def pick_pair(first, second, odd_first, odd_second):
    low = lax.broadcasted_iota(jnp.int32, first.shape, 1) < BLOCK
    a = jnp.where(odd_first, pltpu.roll(first, BLOCK, 1), first)
    b = jnp.where(odd_second, second, pltpu.roll(second, BLOCK, 1))
    return jnp.where(low, a, b)


def columns_kernel(groups, ids_ref, w_ref, out_ref):
    _, c, k = place()
    for p in range(groups):
        tile = ((c ^ p) << 1) + k
        for pair in range(SLOTS // 2):
            windows = []
            odds = []
            for slot in (2 * pair, 2 * pair + 1):
                block = ids_ref[tile, slot]
                start = pl.multiple_of((block >> 1) * LANES, LANES)
                windows.append(w_ref[:, pl.ds(start, LANES)])
                odds.append((block & 1) == 1)
            picked = pick_pair(windows[0].astype(F32), windows[1].astype(F32), *odds)
            out_ref[p, :, pair * LANES : (pair + 1) * LANES] = picked.astype(BF16)


def rows_kernel(groups, ids_ref, own_ref, oth_ref, own_rows, oth_rows, sems):
    _, c, k = place()
    copies = []
    for p in range(groups):
        tile = ((c ^ p) << 1) + k
        for slot in range(SLOTS):
            rows = pl.ds(pl.multiple_of(ids_ref[tile, slot] * BLOCK, BLOCK), BLOCK)
            into = pl.ds(slot * BLOCK, BLOCK)
            for which, (src, dst) in enumerate(((own_ref, own_rows), (oth_ref, oth_rows))):
                copy = pltpu.make_async_copy(
                    src.at[rows, :], dst.at[p, into, :], sems.at[p, slot, which]
                )
                copy.start()
                copies.append(copy)
    for copy in copies:
        copy.wait()


def encode_kernel(groups, *refs):
    pieces, (own_ref, oth_ref, out_ref) = refs[:groups], refs[groups:]
    for p in range(groups):
        acc = jnp.dot(pieces[p][0], own_ref[p], preferred_element_type=F32)
        acc += jnp.dot(pieces[p][1], oth_ref[p], preferred_element_type=F32)
        out_ref[p] = acc.astype(BF16)


def decode_kernel(groups, *refs):
    ids_ref, counts_ref, bias_ref = refs[:3]
    parts = refs[3 : 3 + groups]
    own_rows, oth_rows = refs[3 + groups : 5 + groups]
    code_ref = refs[5 + groups]
    outs = refs[6 + groups :]
    _, c, k = place()
    lane = lax.broadcasted_iota(jnp.int32, (1, LANES), 1)
    for p in range(groups):
        tile = ((c ^ p) << 1) + k
        count = counts_ref[tile]
        code = []
        for pair in range(SLOTS // 2):
            cols = slice(pair * LANES, (pair + 1) * LANES)
            pre = parts[0][p, :, cols].astype(F32)
            for q in range(1, groups):
                pre += parts[q][p ^ q, :, cols].astype(F32)
            bias = []
            odds = []
            for slot in (2 * pair, 2 * pair + 1):
                block = ids_ref[tile, slot]
                bias.append(bias_ref[pl.ds(block >> 1, 1), :])
                odds.append((block & 1) == 1)
            row = pick_pair(bias[0], bias[1], *odds)
            live = (lane >= BLOCK).astype(jnp.int32) + 2 * pair < count
            value = jnp.where(live, jnp.maximum(pre + row, 0.0), 0.0).astype(BF16)
            code.append(value)
        code = jnp.concatenate(code, axis=1)
        if p == 0:
            code_ref[...] = code
        outs[p][k] = jnp.dot(code, own_rows[p], preferred_element_type=F32).astype(BF16)
        outs[p][1 - k] = jnp.dot(code, oth_rows[p], preferred_element_type=F32).astype(BF16)


def route_kernel(groups, *refs):
    came, outs, held = refs[:groups], refs[groups : 2 * groups], refs[2 * groups]
    f, c, _ = place()
    for p in range(groups):
        held[p] = came[p][...]
    for m in range(groups):
        outs[m][...] = held[c ^ f ^ m]


def finish_kernel(groups, chunks, *refs):
    arrived, (bias_ref, out_ref) = refs[: groups * chunks], refs[groups * chunks :]
    f, _, _ = place()
    _, rows, wslice = arrived[0].shape
    for h in range(chunks):
        for half in range(2):
            total = arrived[h * groups][half].astype(F32)
            for ref in arrived[h * groups + 1 : (h + 1) * groups]:
                total += ref[half].astype(F32)
            total += bias_ref[pl.ds(2 * f + half, 1), :]
            out_ref[h * rows : (h + 1) * rows, half * wslice : (half + 1) * wslice] = (
                total.astype(BF16)
            )


def on_device(tokens, dec_bias, enc_weight, enc_bias, dec_weight, block_ids, block_counts):
    tile_count = lax.axis_size("tok")
    groups = lax.axis_size("feat")
    tok_rows, width = tokens.shape
    wslice = width // tile_count
    feats = enc_weight.shape[1]
    rows = tok_rows // CHUNKS
    ids = block_ids[:, 0, :]
    counts = block_counts[:, 0]
    bias_rows = dec_bias.astype(F32).reshape(tile_count, wslice)
    enc_bias_rows = enc_bias.astype(F32).reshape(feats // LANES, LANES)

    def swap(value, p):
        pairs = [(i, i ^ (2 * p)) for i in range(tile_count)]
        return lax.ppermute(value, "tok", pairs)

    def lift(value, m):
        return lax.ppermute(value, "feat", [(i, i ^ m) for i in range(groups)])

    cores = [(i, i ^ 1) for i in range(tile_count)]
    enc_other = lax.ppermute(enc_weight, "tok", cores)
    dec_other = lax.ppermute(dec_weight, "tok", cores)

    piece = jax.ShapeDtypeStruct((2, rows, wslice), BF16)
    sent = pl.pallas_call(
        functools.partial(center_kernel, groups, wslice, CHUNKS),
        out_shape=[piece] * (groups * CHUNKS),
        in_specs=[spec(VMEM)] * 2,
        out_specs=[spec(VMEM)] * (groups * CHUNKS),
        compiler_params=params(8),
        cost_estimate=cost(width * tok_rows, 4 * width * tok_rows),
        name="center",
    )(tokens, bias_rows)

    def columns(weight):
        return pl.pallas_call(
            functools.partial(columns_kernel, groups),
            out_shape=jax.ShapeDtypeStruct((groups, wslice, ACTIVE), BF16),
            in_specs=[spec(SMEM), spec(VMEM)],
            out_specs=spec(VMEM),
            compiler_params=params(8),
            cost_estimate=cost(0, 2 * wslice * (feats + groups * ACTIVE)),
            name="columns",
        )(ids, weight)

    own_cols = columns(enc_weight)
    oth_cols = columns(enc_other)

    listed = jax.ShapeDtypeStruct((groups, ACTIVE, wslice), BF16)
    own_rows, oth_rows = pl.pallas_call(
        functools.partial(rows_kernel, groups),
        out_shape=[listed] * 2,
        in_specs=[spec(SMEM)] + [spec(pl.ANY)] * 2,
        out_specs=[spec(VMEM)] * 2,
        scratch_shapes=[pltpu.SemaphoreType.DMA((groups, SLOTS, 2))],
        compiler_params=params(8),
        cost_estimate=cost(0, 8 * groups * ACTIVE * wslice),
        name="rows",
    )(ids, dec_weight, dec_other)

    flops = 4 * groups * rows * wslice * ACTIVE
    codes = []
    arrived = []
    for h in range(CHUNKS):
        first = sent[h * groups : (h + 1) * groups]
        pieces = [first[0]] + [swap(first[p], p) for p in range(1, groups)]
        part = pl.pallas_call(
            functools.partial(encode_kernel, groups),
            out_shape=jax.ShapeDtypeStruct((groups, rows, ACTIVE), BF16),
            in_specs=[spec(VMEM)] * (groups + 2),
            out_specs=spec(VMEM),
            compiler_params=params(8),
            cost_estimate=cost(flops, 4 * groups * wslice * ACTIVE),
            name="encode",
        )(*pieces, own_cols, oth_cols)
        parts = [part] + [swap(part, p) for p in range(1, groups)]
        decoded = pl.pallas_call(
            functools.partial(decode_kernel, groups),
            out_shape=[jax.ShapeDtypeStruct((rows, ACTIVE), BF16)] + [piece] * groups,
            in_specs=[spec(SMEM)] * 2 + [spec(VMEM)] * (3 + groups),
            out_specs=[spec(VMEM)] * (1 + groups),
            compiler_params=params(8),
            cost_estimate=cost(flops, 4 * groups * wslice * ACTIVE),
            name="decode",
        )(ids, counts, enc_bias_rows, *parts, own_rows, oth_rows)
        codes.append(decoded[0])
        came = [decoded[1]] + [swap(decoded[1 + p], p) for p in range(1, groups)]
        routed = pl.pallas_call(
            functools.partial(route_kernel, groups),
            out_shape=[piece] * groups,
            in_specs=[spec(VMEM)] * groups,
            out_specs=[spec(VMEM)] * groups,
            scratch_shapes=[VMEM((groups, 2, rows, wslice), BF16)],
            compiler_params=params(8),
            cost_estimate=cost(0, 8 * groups * rows * wslice),
            name="route",
        )(*came)
        arrived += [routed[0]] + [lift(routed[m], m) for m in range(1, groups)]

    rebuilt = pl.pallas_call(
        functools.partial(finish_kernel, groups, CHUNKS),
        out_shape=jax.ShapeDtypeStruct((tok_rows, 2 * wslice), BF16),
        in_specs=[spec(VMEM)] * (groups * CHUNKS + 1),
        out_specs=spec(VMEM),
        compiler_params=params(8),
        cost_estimate=cost(0, 4 * (groups + 1) * tok_rows * wslice),
        name="finish",
    )(*arrived, bias_rows)
    return (jnp.concatenate(codes, axis=0), rebuilt)


def solution(mesh):
    in_specs = (
        P("tok", None),
        P(),
        P("tok", "feat"),
        P("feat"),
        P("feat", "tok"),
        P(None, "feat", None),
        P(None, "feat"),
    )
    out_specs = (P("tok", "feat"), P("tok", "feat"))
    return jax.shard_map(
        on_device, mesh=mesh, in_specs=in_specs, out_specs=out_specs, check_vma=False
    )
```

```python
import functools

import jax
import jax.numpy as jnp
from jax import lax
from jax.experimental import pallas as pl
from jax.experimental.pallas import tpu as pltpu
from jax.sharding import PartitionSpec as P

BLOCK = 64
SLOTS = 4
LANES = 128
ACTIVE = SLOTS * BLOCK
CHUNKS = 2
VMEM = pltpu.VMEM
SMEM = pltpu.SMEM
HBM = pltpu.HBM
BF16 = jnp.bfloat16
F32 = jnp.float32


def spec(space):
    return pl.BlockSpec(memory_space=space)


def params(mib):
    return pltpu.CompilerParams(vmem_limit_bytes=mib << 20)


def cost(flops, nbytes):
    return pl.CostEstimate(flops=flops, bytes_accessed=nbytes, transcendentals=0)


def pin(value):
    return pltpu.with_memory_space_constraint(value, HBM)


def place():
    tok = lax.axis_index("tok")
    return lax.axis_index("feat"), tok >> 1, tok & 1


def split_kernel(groups, tok_ref, *refs):
    outs, sems = refs[:-1], refs[-1]
    _, c, k = place()
    wslice = outs[0].shape[2]
    copies = []
    for p in range(groups):
        for half in range(2):
            u = ((c ^ p) << 1) + (k ^ half)
            cols = pl.ds(pl.multiple_of(u * wslice, wslice), wslice)
            copy = pltpu.make_async_copy(
                tok_ref.at[:, cols], outs[p].at[half], sems.at[p, half]
            )
            copy.start()
            copies.append(copy)
    for copy in copies:
        copy.wait()


def pick_pair(first, second, odd_first, odd_second):
    low = lax.broadcasted_iota(jnp.int32, first.shape, 1) < BLOCK
    a = jnp.where(odd_first, pltpu.roll(first, BLOCK, 1), first)
    b = jnp.where(odd_second, second, pltpu.roll(second, BLOCK, 1))
    return jnp.where(low, a, b)


def columns_kernel(groups, ids_ref, w_ref, out_ref):
    _, c, k = place()
    for p in range(groups):
        tile = ((c ^ p) << 1) + k
        for pair in range(SLOTS // 2):
            windows = []
            odds = []
            for slot in (2 * pair, 2 * pair + 1):
                block = ids_ref[tile, slot]
                start = pl.multiple_of((block >> 1) * LANES, LANES)
                windows.append(w_ref[:, pl.ds(start, LANES)])
                odds.append((block & 1) == 1)
            picked = pick_pair(windows[0].astype(F32), windows[1].astype(F32), *odds)
            out_ref[p, :, pair * LANES : (pair + 1) * LANES] = picked.astype(BF16)


def stage_kernel(src, dst, sems):
    parts = sems.shape[0]
    height = src.shape[0] // parts
    copies = []
    for i in range(parts):
        some = pl.ds(i * height, height)
        copy = pltpu.make_async_copy(src.at[some, :], dst.at[some, :], sems.at[i])
        copy.start()
        copies.append(copy)
    for copy in copies:
        copy.wait()


def encode_kernel(groups, *refs):
    bias_ref, pieces, (own_ref, oth_ref, out_ref) = refs[0], refs[1 : 1 + groups], refs[1 + groups :]
    _, c, k = place()
    bias = [bias_ref[pl.ds(2 * c + (k ^ half), 1), :] for half in range(2)]
    for p in range(groups):
        mine, other = [
            (pieces[p][half].astype(F32) - bias[half]).astype(BF16) for half in range(2)
        ]
        acc = jnp.dot(mine, own_ref[p], preferred_element_type=F32)
        acc += jnp.dot(other, oth_ref[p], preferred_element_type=F32)
        out_ref[p] = acc.astype(BF16)


def decode_kernel(groups, chunks, *refs):
    ids_ref, counts_ref, bias_ref = refs[:3]
    parts = refs[3 : 3 + groups]
    own_ref, oth_ref, code_ref = refs[3 + groups : 6 + groups]
    outs = refs[6 + groups :]
    _, c, k = place()
    lane = lax.broadcasted_iota(jnp.int32, (1, LANES), 1)
    for p in range(groups):
        tile = ((c ^ p) << 1) + k
        count = counts_ref[tile]
        code = []
        listed = []
        for pair in range(SLOTS // 2):
            cols = slice(pair * LANES, (pair + 1) * LANES)
            pre = parts[0][p, :, cols].astype(F32)
            for q in range(1, groups):
                pre += parts[q][p ^ q, :, cols].astype(F32)
            bias = []
            odds = []
            for slot in (2 * pair, 2 * pair + 1):
                block = ids_ref[tile, slot]
                listed.append(pl.ds(pl.multiple_of(block * BLOCK, BLOCK), BLOCK))
                bias.append(bias_ref[pl.ds(block >> 1, 1), :])
                odds.append((block & 1) == 1)
            row = pick_pair(bias[0], bias[1], *odds)
            live = (lane >= BLOCK).astype(jnp.int32) + 2 * pair < count
            value = jnp.where(live, jnp.maximum(pre + row, 0.0), 0.0).astype(BF16)
            code.append(value)
        code = jnp.concatenate(code, axis=1)
        if p == 0:
            code_ref[...] = code
        height = code.shape[0] // chunks
        for half, ref in ((k, own_ref), (1 - k, oth_ref)):
            rows = jnp.concatenate([ref[some, :] for some in listed], axis=0)
            result = jnp.dot(code, rows, preferred_element_type=F32).astype(BF16)
            for h in range(chunks):
                outs[h * groups + p][half] = result[h * height : (h + 1) * height]


def route_kernel(groups, *refs):
    came, (keep_ref, send_ref, held) = refs[:groups], refs[groups:]
    f, c, _ = place()
    for p in range(groups):
        held[p] = came[p][...]
    for m in range(0, groups, 2):
        keep_ref[m // 2] = held[c ^ f ^ m]
        send_ref[m // 2] = held[c ^ f ^ m ^ 1]


def add_kernel(groups, keep_ref, came_ref, *outs):
    for i in range(1, groups // 2):
        total = keep_ref[i].astype(F32) + came_ref[i].astype(F32)
        outs[i - 1][...] = total.astype(BF16)


def finish_kernel(groups, chunks, *refs):
    bias_ref, out_ref = refs[-2:]
    each = 1 + groups // 2
    f, _, _ = place()
    for h in range(chunks):
        keep_ref, came_ref, *far = refs[h * each : (h + 1) * each]
        _, _, rows, wslice = keep_ref.shape
        for half in range(2):
            total = keep_ref[0, half].astype(F32) + came_ref[0, half].astype(F32)
            for ref in far:
                total += ref[half].astype(F32)
            total += bias_ref[pl.ds(2 * f + half, 1), :]
            out_ref[h * rows : (h + 1) * rows, half * wslice : (half + 1) * wslice] = (
                total.astype(BF16)
            )


def on_device(tokens, dec_bias, enc_weight, enc_bias, dec_weight, block_ids, block_counts):
    tile_count = lax.axis_size("tok")
    groups = lax.axis_size("feat")
    tok_rows, width = tokens.shape
    wslice = width // tile_count
    feats = enc_weight.shape[1]
    rows = tok_rows // CHUNKS
    ids = block_ids[:, 0, :]
    counts = block_counts[:, 0]
    bias_rows = dec_bias.astype(F32).reshape(tile_count, wslice)
    enc_bias_rows = enc_bias.astype(F32).reshape(feats // LANES, LANES)

    def swap(value, p):
        pairs = [(i, i ^ (2 * p)) for i in range(tile_count)]
        return lax.ppermute(value, "tok", pairs)

    def lift(value, m):
        return lax.ppermute(value, "feat", [(i, i ^ m) for i in range(groups)])

    cores = [(i, i ^ 1) for i in range(tile_count)]
    enc_other = lax.ppermute(enc_weight, "tok", cores)
    dec_other = lax.ppermute(dec_weight, "tok", cores)

    sent = pl.pallas_call(
        functools.partial(split_kernel, groups),
        out_shape=[jax.ShapeDtypeStruct((2, tok_rows, wslice), BF16)] * groups,
        in_specs=[spec(pl.ANY)],
        out_specs=[spec(VMEM)] * groups,
        scratch_shapes=[pltpu.SemaphoreType.DMA((groups, 2))],
        compiler_params=params(8),
        cost_estimate=cost(0, 4 * width * tok_rows),
        name="split",
    )(pin(tokens))
    pieces = [sent[0]] + [swap(sent[p], p) for p in range(1, groups)]

    chunk = min(wslice, 256)

    def columns(weight):
        return pl.pallas_call(
            functools.partial(columns_kernel, groups),
            out_shape=jax.ShapeDtypeStruct((groups, wslice, ACTIVE), BF16),
            grid=(wslice // chunk,),
            in_specs=[spec(SMEM), pl.BlockSpec((chunk, feats), lambda i: (i, 0))],
            out_specs=pl.BlockSpec((groups, chunk, ACTIVE), lambda i: (0, i, 0)),
            compiler_params=params(16),
            cost_estimate=cost(0, 2 * wslice * (feats + groups * ACTIVE)),
            name="columns",
        )(ids, weight)

    own_cols = columns(enc_weight)
    oth_cols = columns(enc_other)
    flops = 4 * groups * tok_rows * wslice * ACTIVE
    part = pl.pallas_call(
        functools.partial(encode_kernel, groups),
        out_shape=jax.ShapeDtypeStruct((groups, tok_rows, ACTIVE), BF16),
        in_specs=[spec(VMEM)] * (groups + 3),
        out_specs=spec(VMEM),
        compiler_params=params(16),
        cost_estimate=cost(flops, 4 * groups * wslice * ACTIVE),
        name="encode",
    )(bias_rows, *pieces, own_cols, oth_cols)
    parts = [part] + [swap(part, p) for p in range(1, groups)]

    dec_staged = pl.pallas_call(
        stage_kernel,
        out_shape=jax.ShapeDtypeStruct(dec_weight.shape, BF16),
        in_specs=[spec(pl.ANY)],
        out_specs=spec(VMEM),
        scratch_shapes=[pltpu.SemaphoreType.DMA((8,))],
        compiler_params=params(8),
        cost_estimate=cost(0, 4 * wslice * feats),
        name="stage",
    )(dec_other)
    piece = jax.ShapeDtypeStruct((2, rows, wslice), BF16)
    decoded = pl.pallas_call(
        functools.partial(decode_kernel, groups, CHUNKS),
        out_shape=[jax.ShapeDtypeStruct((tok_rows, ACTIVE), BF16)]
        + [piece] * (groups * CHUNKS),
        in_specs=[spec(SMEM)] * 2 + [spec(VMEM)] * (3 + groups),
        out_specs=[spec(VMEM)] * (1 + groups * CHUNKS),
        compiler_params=params(16),
        cost_estimate=cost(flops, 4 * groups * wslice * ACTIVE),
        name="decode",
    )(ids, counts, enc_bias_rows, *parts, dec_weight, dec_staged)

    both = jax.ShapeDtypeStruct((groups // 2, 2, rows, wslice), BF16)
    moved = []
    for h in range(CHUNKS):
        made = decoded[1 + h * groups : 1 + (h + 1) * groups]
        came = [made[0]] + [swap(made[p], p) for p in range(1, groups)]
        keep, send = pl.pallas_call(
            functools.partial(route_kernel, groups),
            out_shape=[both] * 2,
            in_specs=[spec(VMEM)] * groups,
            out_specs=[spec(VMEM)] * 2,
            scratch_shapes=[VMEM((groups, 2, rows, wslice), BF16)],
            compiler_params=params(8),
            cost_estimate=cost(0, 8 * groups * rows * wslice),
            name="route",
        )(*came)
        near = lift(send, 1)
        sums = pl.pallas_call(
            functools.partial(add_kernel, groups),
            out_shape=[piece] * (groups // 2 - 1),
            in_specs=[spec(VMEM)] * 2,
            out_specs=[spec(VMEM)] * (groups // 2 - 1),
            compiler_params=params(8),
            cost_estimate=cost(groups * rows * wslice, 6 * groups * rows * wslice),
            name="add",
        )(keep, near)
        moved += [keep, near] + [lift(sums[m // 2 - 1], m) for m in range(2, groups, 2)]

    rebuilt = pl.pallas_call(
        functools.partial(finish_kernel, groups, CHUNKS),
        out_shape=jax.ShapeDtypeStruct((tok_rows, 2 * wslice), BF16),
        in_specs=[spec(VMEM)] * (len(moved) + 1),
        out_specs=spec(VMEM),
        compiler_params=params(8),
        cost_estimate=cost(0, 4 * (groups + 1) * tok_rows * wslice),
        name="finish",
    )(*moved, bias_rows)
    return (decoded[0], rebuilt)


def solution(mesh):
    in_specs = (
        P("tok", None),
        P(),
        P("tok", "feat"),
        P("feat"),
        P("feat", "tok"),
        P(None, "feat", None),
        P(None, "feat"),
    )
    out_specs = (P("tok", "feat"), P("tok", "feat"))
    return jax.shard_map(
        on_device, mesh=mesh, in_specs=in_specs, out_specs=out_specs, check_vma=False
    )
```

```python
import functools

import jax
import jax.numpy as jnp
from jax import lax
from jax.experimental import pallas as pl
from jax.experimental.pallas import tpu as pltpu
from jax.sharding import PartitionSpec as P

BLOCK = 64
SLOTS = 4
LANES = 128
ACTIVE = SLOTS * BLOCK
VMEM = pltpu.VMEM
SMEM = pltpu.SMEM
HBM = pltpu.HBM
BF16 = jnp.bfloat16
F32 = jnp.float32


def spec(space):
    return pl.BlockSpec(memory_space=space)


def params(mib):
    return pltpu.CompilerParams(vmem_limit_bytes=mib << 20)


def cost(flops, nbytes):
    return pl.CostEstimate(flops=flops, bytes_accessed=nbytes, transcendentals=0)


def pin(value):
    return pltpu.with_memory_space_constraint(value, HBM)


def place():
    tok = lax.axis_index("tok")
    return lax.axis_index("feat"), tok >> 1, tok & 1


def split_kernel(groups, tok_ref, *outs):
    _, c, k = place()
    wslice = outs[0].shape[2]
    for p in range(groups):
        for half in range(2):
            u = ((c ^ p) << 1) + (k ^ half)
            cols = pl.ds(pl.multiple_of(u * wslice, wslice), wslice)
            outs[p][half] = tok_ref[:, cols]


def pick_pair(first, second, odd_first, odd_second):
    low = lax.broadcasted_iota(jnp.int32, first.shape, 1) < BLOCK
    a = jnp.where(odd_first, pltpu.roll(first, BLOCK, 1), first)
    b = jnp.where(odd_second, second, pltpu.roll(second, BLOCK, 1))
    return jnp.where(low, a, b)


def columns_kernel(groups, ids_ref, w_ref, out_ref):
    _, c, k = place()
    for p in range(groups):
        tile = ((c ^ p) << 1) + k
        for pair in range(SLOTS // 2):
            windows = []
            odds = []
            for slot in (2 * pair, 2 * pair + 1):
                block = ids_ref[tile, slot]
                start = pl.multiple_of((block >> 1) * LANES, LANES)
                windows.append(w_ref[:, pl.ds(start, LANES)])
                odds.append((block & 1) == 1)
            picked = pick_pair(windows[0].astype(F32), windows[1].astype(F32), *odds)
            out_ref[p, :, pair * LANES : (pair + 1) * LANES] = picked.astype(BF16)


def stage_kernel(src, dst, sems):
    parts = sems.shape[0]
    height = src.shape[0] // parts
    copies = []
    for i in range(parts):
        some = pl.ds(i * height, height)
        copy = pltpu.make_async_copy(src.at[some, :], dst.at[some, :], sems.at[i])
        copy.start()
        copies.append(copy)
    for copy in copies:
        copy.wait()


def encode_kernel(groups, *refs):
    bias_ref, pieces, (own_ref, oth_ref, out_ref) = refs[0], refs[1 : 1 + groups], refs[1 + groups :]
    _, c, k = place()
    bias = [bias_ref[pl.ds(2 * c + (k ^ half), 1), :] for half in range(2)]
    for p in range(groups):
        mine, other = [
            (pieces[p][half].astype(F32) - bias[half]).astype(BF16) for half in range(2)
        ]
        acc = jnp.dot(mine, own_ref[p], preferred_element_type=F32)
        acc += jnp.dot(other, oth_ref[p], preferred_element_type=F32)
        out_ref[p] = acc.astype(BF16)


def decode_kernel(groups, *refs):
    ids_ref, counts_ref, bias_ref = refs[:3]
    parts = refs[3 : 3 + groups]
    own_ref, oth_ref, code_ref = refs[3 + groups : 6 + groups]
    firsts = refs[6 + groups : 6 + 2 * groups]
    keep_ref, send_ref = refs[6 + 2 * groups :]
    f, c, k = place()
    even = (f & 1) == 0
    lane = lax.broadcasted_iota(jnp.int32, (1, LANES), 1)
    for p in range(groups):
        tile = ((c ^ p) << 1) + k
        count = counts_ref[tile]
        code = []
        listed = []
        for pair in range(SLOTS // 2):
            cols = slice(pair * LANES, (pair + 1) * LANES)
            pre = parts[0][p, :, cols].astype(F32)
            for q in range(1, groups):
                pre += parts[q][p ^ q, :, cols].astype(F32)
            bias = []
            odds = []
            for slot in (2 * pair, 2 * pair + 1):
                block = ids_ref[tile, slot]
                listed.append(pl.ds(pl.multiple_of(block * BLOCK, BLOCK), BLOCK))
                bias.append(bias_ref[pl.ds(block >> 1, 1), :])
                odds.append((block & 1) == 1)
            row = pick_pair(bias[0], bias[1], *odds)
            live = (lane >= BLOCK).astype(jnp.int32) + 2 * pair < count
            value = jnp.where(live, jnp.maximum(pre + row, 0.0), 0.0).astype(BF16)
            code.append(value)
        code = jnp.concatenate(code, axis=1)
        if p == 0:
            code_ref[...] = code
        height = code.shape[0] // 4
        for half, ref in ((k, own_ref), (1 - k, oth_ref)):
            rows = jnp.concatenate([ref[some, :] for some in listed], axis=0)
            result = jnp.dot(code, rows, preferred_element_type=F32).astype(BF16)
            firsts[p][half] = result[: 2 * height]
            third, fourth = result[2 * height : 3 * height], result[3 * height :]
            keep_ref[p, half] = jnp.where(even, third, fourth)
            send_ref[p, half] = jnp.where(even, fourth, third)


def route_kernel(groups, *refs):
    came, (keep_ref, send_ref, held) = refs[:groups], refs[groups:]
    f, c, _ = place()
    for p in range(groups):
        held[p] = came[p][...]
    for m in range(0, groups, 2):
        keep_ref[m // 2] = held[c ^ f ^ m]
        send_ref[m // 2] = held[c ^ f ^ m ^ 1]


def add_kernel(groups, keep_ref, came_ref, *outs):
    for i in range(1, groups // 2):
        total = keep_ref[i].astype(F32) + came_ref[i].astype(F32)
        outs[i - 1][...] = total.astype(BF16)


def merge_kernel(groups, keep_ref, came_ref, *outs):
    for p in range(groups):
        outs[p][...] = (keep_ref[p].astype(F32) + came_ref[p].astype(F32)).astype(BF16)


def direct_kernel(groups, *refs):
    came, outs, held = refs[:groups], refs[groups : 2 * groups], refs[2 * groups]
    f, c, _ = place()
    for p in range(groups):
        held[p] = came[p][...]
    for m in range(groups):
        outs[m][...] = held[c ^ f ^ m]


def finish_kernel(groups, *refs):
    bias_ref, out_ref = refs[-2:]
    keep_ref, came_ref, *far = refs[: 1 + groups // 2]
    direct = refs[1 + groups // 2 : -2]
    f, _, _ = place()
    _, rows, wslice = direct[0].shape
    for half in range(2):
        cols = slice(half * wslice, (half + 1) * wslice)
        bias = bias_ref[pl.ds(2 * f + half, 1), :]
        total = keep_ref[0, half].astype(F32) + came_ref[0, half].astype(F32)
        for ref in far:
            total += ref[half].astype(F32)
        out_ref[: 2 * rows, cols] = (total + bias).astype(BF16)
        for odd in range(2):
            total = direct[odd][half].astype(F32)
            for ref in direct[2 + odd :: 2]:
                total += ref[half].astype(F32)
            start = pl.multiple_of(2 * rows + ((f & 1) ^ odd) * rows, rows)
            out_ref[pl.ds(start, rows), cols] = (total + bias).astype(BF16)


def on_device(tokens, dec_bias, enc_weight, enc_bias, dec_weight, block_ids, block_counts):
    tile_count = lax.axis_size("tok")
    groups = lax.axis_size("feat")
    tok_rows, width = tokens.shape
    wslice = width // tile_count
    feats = enc_weight.shape[1]
    ids = block_ids[:, 0, :]
    counts = block_counts[:, 0]
    bias_rows = dec_bias.astype(F32).reshape(tile_count, wslice)
    enc_bias_rows = enc_bias.astype(F32).reshape(feats // LANES, LANES)

    def swap(value, p):
        pairs = [(i, i ^ (2 * p)) for i in range(tile_count)]
        return lax.ppermute(value, "tok", pairs)

    def lift(value, m):
        return lax.ppermute(value, "feat", [(i, i ^ m) for i in range(groups)])

    cores = [(i, i ^ 1) for i in range(tile_count)]
    enc_other = lax.ppermute(enc_weight, "tok", cores)
    dec_other = lax.ppermute(dec_weight, "tok", cores)

    sent = pl.pallas_call(
        functools.partial(split_kernel, groups),
        out_shape=[jax.ShapeDtypeStruct((2, tok_rows, wslice), BF16)] * groups,
        in_specs=[spec(VMEM)],
        out_specs=[spec(VMEM)] * groups,
        compiler_params=params(8),
        cost_estimate=cost(0, 4 * width * tok_rows),
        name="split",
    )(tokens)
    pieces = [sent[0]] + [swap(sent[p], p) for p in range(1, groups)]

    chunk = min(wslice, 256)

    def columns(weight):
        return pl.pallas_call(
            functools.partial(columns_kernel, groups),
            out_shape=jax.ShapeDtypeStruct((groups, wslice, ACTIVE), BF16),
            grid=(wslice // chunk,),
            in_specs=[spec(SMEM), pl.BlockSpec((chunk, feats), lambda i: (i, 0))],
            out_specs=pl.BlockSpec((groups, chunk, ACTIVE), lambda i: (0, i, 0)),
            compiler_params=params(8),
            cost_estimate=cost(0, 2 * wslice * (feats + groups * ACTIVE)),
            name="columns",
        )(ids, weight)

    own_cols = columns(enc_weight)
    oth_cols = columns(enc_other)
    flops = 4 * groups * tok_rows * wslice * ACTIVE
    part = pl.pallas_call(
        functools.partial(encode_kernel, groups),
        out_shape=jax.ShapeDtypeStruct((groups, tok_rows, ACTIVE), BF16),
        in_specs=[spec(VMEM)] * (groups + 3),
        out_specs=spec(VMEM),
        compiler_params=params(8),
        cost_estimate=cost(flops, 4 * groups * wslice * ACTIVE),
        name="encode",
    )(bias_rows, *pieces, own_cols, oth_cols)
    parts = [part] + [swap(part, p) for p in range(1, groups)]

    dec_staged = pl.pallas_call(
        stage_kernel,
        out_shape=jax.ShapeDtypeStruct(dec_weight.shape, BF16),
        in_specs=[spec(pl.ANY)],
        out_specs=spec(VMEM),
        scratch_shapes=[pltpu.SemaphoreType.DMA((8,))],
        compiler_params=params(8),
        cost_estimate=cost(0, 4 * wslice * feats),
        name="stage",
    )(dec_other)
    half_rows = tok_rows // 2
    quarter_rows = tok_rows // 4
    piece = jax.ShapeDtypeStruct((2, half_rows, wslice), BF16)
    small = jax.ShapeDtypeStruct((2, quarter_rows, wslice), BF16)
    smalls = jax.ShapeDtypeStruct((groups, 2, quarter_rows, wslice), BF16)
    code_values, *outgoing = pl.pallas_call(
        functools.partial(decode_kernel, groups),
        out_shape=[jax.ShapeDtypeStruct((tok_rows, ACTIVE), BF16)]
        + [piece] * groups
        + [smalls] * 2,
        in_specs=[spec(SMEM)] * 2 + [spec(VMEM)] * (3 + groups),
        out_specs=[spec(VMEM)] * (3 + groups),
        compiler_params=params(8),
        cost_estimate=cost(flops, 4 * groups * wslice * ACTIVE),
        name="decode",
    )(ids, counts, enc_bias_rows, *parts, dec_weight, dec_staged)
    firsts, (own_sums, sent_sums) = outgoing[:groups], outgoing[groups:]

    swapped = lift(sent_sums, 1)
    came = [firsts[0]] + [swap(firsts[p], p) for p in range(1, groups)]
    both = jax.ShapeDtypeStruct((groups // 2,) + piece.shape, BF16)
    keep, send = pl.pallas_call(
        functools.partial(route_kernel, groups),
        out_shape=[both] * 2,
        in_specs=[spec(VMEM)] * groups,
        out_specs=[spec(VMEM)] * 2,
        scratch_shapes=[VMEM((groups,) + piece.shape, BF16)],
        compiler_params=params(8),
        cost_estimate=cost(0, 8 * groups * half_rows * wslice),
        name="route",
    )(*came)
    near = lift(send, 1)
    merged = pl.pallas_call(
        functools.partial(merge_kernel, groups),
        out_shape=[small] * groups,
        in_specs=[spec(VMEM)] * 2,
        out_specs=[spec(VMEM)] * groups,
        compiler_params=params(8),
        cost_estimate=cost(0, 8 * groups * quarter_rows * wslice),
        name="merge",
    )(own_sums, swapped)
    merged = [merged[0]] + [swap(merged[p], p) for p in range(1, groups)]
    direct = pl.pallas_call(
        functools.partial(direct_kernel, groups),
        out_shape=[small] * groups,
        in_specs=[spec(VMEM)] * groups,
        out_specs=[spec(VMEM)] * groups,
        scratch_shapes=[VMEM((groups,) + small.shape, BF16)],
        compiler_params=params(8),
        cost_estimate=cost(0, 8 * groups * quarter_rows * wslice),
        name="direct",
    )(*merged)
    sums = pl.pallas_call(
        functools.partial(add_kernel, groups),
        out_shape=[piece] * (groups // 2 - 1),
        in_specs=[spec(VMEM)] * 2,
        out_specs=[spec(VMEM)] * (groups // 2 - 1),
        compiler_params=params(8),
        cost_estimate=cost(groups * half_rows * wslice, 6 * groups * half_rows * wslice),
        name="add",
    )(keep, near)
    moved = [keep, near] + [lift(sums[m // 2 - 1], m) for m in range(2, groups, 2)]
    moved += [direct[0]] + [lift(direct[m], m) for m in range(1, groups)]

    rebuilt = pl.pallas_call(
        functools.partial(finish_kernel, groups),
        out_shape=jax.ShapeDtypeStruct((tok_rows, 2 * wslice), BF16),
        in_specs=[spec(VMEM)] * (len(moved) + 1),
        out_specs=spec(VMEM),
        compiler_params=params(8),
        cost_estimate=cost(0, 4 * (groups + 1) * tok_rows * wslice),
        name="finish",
    )(*moved, bias_rows)
    return (code_values, rebuilt)


def solution(mesh):
    in_specs = (
        P("tok", None),
        P(),
        P("tok", "feat"),
        P("feat"),
        P("feat", "tok"),
        P(None, "feat", None),
        P(None, "feat"),
    )
    out_specs = (P("tok", "feat"), P("tok", "feat"))
    return jax.shard_map(
        on_device, mesh=mesh, in_specs=in_specs, out_specs=out_specs, check_vma=False
    )
```

```python
import functools

import jax
import jax.numpy as jnp
from jax import lax
from jax.experimental import pallas as pl
from jax.experimental.pallas import tpu as pltpu
from jax.sharding import PartitionSpec as P

BLOCK = 64
SLOTS = 4
LANES = 128
ACTIVE = SLOTS * BLOCK
VMEM = pltpu.VMEM
SMEM = pltpu.SMEM
HBM = pltpu.HBM
BF16 = jnp.bfloat16
F32 = jnp.float32


def spec(space):
    return pl.BlockSpec(memory_space=space)


def params(mib):
    return pltpu.CompilerParams(vmem_limit_bytes=mib << 20)


def cost(flops, nbytes):
    return pl.CostEstimate(flops=flops, bytes_accessed=nbytes, transcendentals=0)


def pin(value):
    return pltpu.with_memory_space_constraint(value, HBM)


def place():
    tok = lax.axis_index("tok")
    return lax.axis_index("feat"), tok >> 1, tok & 1


def split_kernel(groups, tok_ref, *outs):
    _, c, k = place()
    wslice = outs[0].shape[2]
    for p in range(groups):
        for half in range(2):
            u = ((c ^ p) << 1) + (k ^ half)
            cols = pl.ds(pl.multiple_of(u * wslice, wslice), wslice)
            outs[p][half] = tok_ref[:, cols]


def pick_pair(first, second, odd_first, odd_second):
    low = lax.broadcasted_iota(jnp.int32, first.shape, 1) < BLOCK
    a = jnp.where(odd_first, pltpu.roll(first, BLOCK, 1), first)
    b = jnp.where(odd_second, second, pltpu.roll(second, BLOCK, 1))
    return jnp.where(low, a, b)


def columns_kernel(groups, ids_ref, w_ref, out_ref):
    _, c, k = place()
    for p in range(groups):
        tile = ((c ^ p) << 1) + k
        for pair in range(SLOTS // 2):
            windows = []
            odds = []
            for slot in (2 * pair, 2 * pair + 1):
                block = ids_ref[tile, slot]
                start = pl.multiple_of((block >> 1) * LANES, LANES)
                windows.append(w_ref[:, pl.ds(start, LANES)])
                odds.append((block & 1) == 1)
            picked = pick_pair(windows[0].astype(F32), windows[1].astype(F32), *odds)
            out_ref[p, :, pair * LANES : (pair + 1) * LANES] = picked.astype(BF16)


def stage_kernel(src, dst, sems):
    parts = sems.shape[0]
    height = src.shape[0] // parts
    copies = []
    for i in range(parts):
        some = pl.ds(i * height, height)
        copy = pltpu.make_async_copy(src.at[some, :], dst.at[some, :], sems.at[i])
        copy.start()
        copies.append(copy)
    for copy in copies:
        copy.wait()


def encode_kernel(groups, *refs):
    bias_ref, pieces, (own_ref, oth_ref, out_ref) = refs[0], refs[1 : 1 + groups], refs[1 + groups :]
    _, c, k = place()
    bias = [bias_ref[pl.ds(2 * c + (k ^ half), 1), :] for half in range(2)]
    for p in range(groups):
        mine, other = [
            (pieces[p][half].astype(F32) - bias[half]).astype(BF16) for half in range(2)
        ]
        acc = jnp.dot(mine, own_ref[p], preferred_element_type=F32)
        acc += jnp.dot(other, oth_ref[p], preferred_element_type=F32)
        out_ref[p] = acc.astype(BF16)


def decode_kernel(groups, *refs):
    ids_ref, counts_ref, bias_ref = refs[:3]
    parts = refs[3 : 3 + groups]
    own_ref, oth_ref, code_ref = refs[3 + groups : 6 + groups]
    firsts = refs[6 + groups : 6 + 2 * groups]
    keep_ref, send_ref = refs[6 + 2 * groups :]
    f, c, k = place()
    even = (f & 1) == 0
    lane = lax.broadcasted_iota(jnp.int32, (1, LANES), 1)
    for p in range(groups):
        tile = ((c ^ p) << 1) + k
        count = counts_ref[tile]
        code = []
        listed = []
        for pair in range(SLOTS // 2):
            cols = slice(pair * LANES, (pair + 1) * LANES)
            pre = parts[0][p, :, cols].astype(F32)
            for q in range(1, groups):
                pre += parts[q][p ^ q, :, cols].astype(F32)
            bias = []
            odds = []
            for slot in (2 * pair, 2 * pair + 1):
                block = ids_ref[tile, slot]
                listed.append(pl.ds(pl.multiple_of(block * BLOCK, BLOCK), BLOCK))
                bias.append(bias_ref[pl.ds(block >> 1, 1), :])
                odds.append((block & 1) == 1)
            row = pick_pair(bias[0], bias[1], *odds)
            live = (lane >= BLOCK).astype(jnp.int32) + 2 * pair < count
            value = jnp.where(live, jnp.maximum(pre + row, 0.0), 0.0).astype(BF16)
            code.append(value)
        code = jnp.concatenate(code, axis=1)
        if p == 0:
            code_ref[...] = code
        height = code.shape[0] // 4
        for half, ref in ((k, own_ref), (1 - k, oth_ref)):
            rows = jnp.concatenate([ref[some, :] for some in listed], axis=0)
            result = jnp.dot(code, rows, preferred_element_type=F32).astype(BF16)
            firsts[p][half] = result[: 2 * height]
            third, fourth = result[2 * height : 3 * height], result[3 * height :]
            keep_ref[p, half] = jnp.where(even, third, fourth)
            send_ref[p, half] = jnp.where(even, fourth, third)


def route_kernel(groups, *refs):
    came, (keep_ref, send_ref, held) = refs[:groups], refs[groups:]
    f, c, _ = place()
    for p in range(groups):
        held[p] = came[p][...]
    for m in range(0, groups, 2):
        keep_ref[m // 2] = held[c ^ f ^ m]
        send_ref[m // 2] = held[c ^ f ^ m ^ 1]


def add_kernel(groups, keep_ref, came_ref, *outs):
    for i in range(1, groups // 2):
        total = keep_ref[i].astype(F32) + came_ref[i].astype(F32)
        outs[i - 1][...] = total.astype(BF16)


def merge_kernel(groups, keep_ref, came_ref, *outs):
    for p in range(groups):
        outs[p][...] = (keep_ref[p].astype(F32) + came_ref[p].astype(F32)).astype(BF16)


def direct_kernel(groups, *refs):
    came, outs, held = refs[:groups], refs[groups : 2 * groups], refs[2 * groups]
    f, c, _ = place()
    for p in range(groups):
        held[p] = came[p][...]
    for m in range(groups):
        outs[m][...] = held[c ^ f ^ m]


def finish_kernel(groups, *refs):
    bias_ref, out_ref = refs[-2:]
    keep_ref, came_ref, *far = refs[: 1 + groups // 2]
    direct = refs[1 + groups // 2 : -2]
    f, _, _ = place()
    _, rows, wslice = direct[0].shape
    for half in range(2):
        cols = slice(half * wslice, (half + 1) * wslice)
        bias = bias_ref[pl.ds(2 * f + half, 1), :]
        total = keep_ref[0, half].astype(F32) + came_ref[0, half].astype(F32)
        for ref in far:
            total += ref[half].astype(F32)
        out_ref[: 2 * rows, cols] = (total + bias).astype(BF16)
        for odd in range(2):
            total = direct[odd][half].astype(F32)
            for ref in direct[2 + odd :: 2]:
                total += ref[half].astype(F32)
            start = pl.multiple_of(2 * rows + ((f & 1) ^ odd) * rows, rows)
            out_ref[pl.ds(start, rows), cols] = (total + bias).astype(BF16)


def on_device(tokens, dec_bias, enc_weight, enc_bias, dec_weight, block_ids, block_counts):
    tile_count = lax.axis_size("tok")
    groups = lax.axis_size("feat")
    tok_rows, width = tokens.shape
    wslice = width // tile_count
    feats = enc_weight.shape[1]
    ids = block_ids[:, 0, :]
    counts = block_counts[:, 0]
    bias_rows = dec_bias.astype(F32).reshape(tile_count, wslice)
    enc_bias_rows = enc_bias.astype(F32).reshape(feats // LANES, LANES)

    def swap(value, p):
        pairs = [(i, i ^ (2 * p)) for i in range(tile_count)]
        return lax.ppermute(value, "tok", pairs)

    def lift(value, m):
        return lax.ppermute(value, "feat", [(i, i ^ m) for i in range(groups)])

    cores = [(i, i ^ 1) for i in range(tile_count)]
    enc_other = lax.ppermute(enc_weight, "tok", cores)
    dec_other = lax.ppermute(dec_weight, "tok", cores)

    sent = pl.pallas_call(
        functools.partial(split_kernel, groups),
        out_shape=[jax.ShapeDtypeStruct((2, tok_rows, wslice), BF16)] * groups,
        in_specs=[spec(VMEM)],
        out_specs=[spec(VMEM)] * groups,
        compiler_params=params(8),
        cost_estimate=cost(0, 4 * width * tok_rows),
        name="split",
    )(tokens)
    pieces = [sent[0]] + [swap(sent[p], p) for p in range(1, groups)]

    chunk = min(wslice, 256)

    def columns(weight):
        return pl.pallas_call(
            functools.partial(columns_kernel, groups),
            out_shape=jax.ShapeDtypeStruct((groups, wslice, ACTIVE), BF16),
            grid=(wslice // chunk,),
            in_specs=[spec(SMEM), pl.BlockSpec((chunk, feats), lambda i: (i, 0))],
            out_specs=pl.BlockSpec((groups, chunk, ACTIVE), lambda i: (0, i, 0)),
            compiler_params=params(8),
            cost_estimate=cost(0, 2 * wslice * (feats + groups * ACTIVE)),
            name="columns",
        )(ids, weight)

    own_cols = columns(enc_weight)
    oth_cols = columns(enc_other)
    flops = 4 * groups * tok_rows * wslice * ACTIVE
    part = pl.pallas_call(
        functools.partial(encode_kernel, groups),
        out_shape=jax.ShapeDtypeStruct((groups, tok_rows, ACTIVE), BF16),
        in_specs=[spec(VMEM)] * (groups + 3),
        out_specs=spec(VMEM),
        compiler_params=params(8),
        cost_estimate=cost(flops, 4 * groups * wslice * ACTIVE),
        name="encode",
    )(bias_rows, *pieces, own_cols, oth_cols)
    parts = [part] + [swap(part, p) for p in range(1, groups)]

    dec_staged = pl.pallas_call(
        stage_kernel,
        out_shape=jax.ShapeDtypeStruct(dec_weight.shape, BF16),
        in_specs=[spec(pl.ANY)],
        out_specs=spec(VMEM),
        scratch_shapes=[pltpu.SemaphoreType.DMA((8,))],
        compiler_params=params(8),
        cost_estimate=cost(0, 4 * wslice * feats),
        name="stage",
    )(dec_other)
    half_rows = tok_rows // 2
    quarter_rows = tok_rows // 4
    piece = jax.ShapeDtypeStruct((2, half_rows, wslice), BF16)
    small = jax.ShapeDtypeStruct((2, quarter_rows, wslice), BF16)
    smalls = jax.ShapeDtypeStruct((groups, 2, quarter_rows, wslice), BF16)
    code_values, *outgoing = pl.pallas_call(
        functools.partial(decode_kernel, groups),
        out_shape=[jax.ShapeDtypeStruct((tok_rows, ACTIVE), BF16)]
        + [piece] * groups
        + [smalls] * 2,
        in_specs=[spec(SMEM)] * 2 + [spec(VMEM)] * (3 + groups),
        out_specs=[spec(VMEM)] * (3 + groups),
        compiler_params=params(8),
        cost_estimate=cost(flops, 4 * groups * wslice * ACTIVE),
        name="decode",
    )(ids, counts, enc_bias_rows, *parts, dec_weight, dec_staged)
    firsts, (own_sums, sent_sums) = outgoing[:groups], outgoing[groups:]

    swapped = lift(sent_sums, 1)
    came = [firsts[0]] + [swap(firsts[p], p) for p in range(1, groups)]
    merged = pl.pallas_call(
        functools.partial(merge_kernel, groups),
        out_shape=[small] * groups,
        in_specs=[spec(VMEM)] * 2,
        out_specs=[spec(VMEM)] * groups,
        compiler_params=params(8),
        cost_estimate=cost(0, 8 * groups * quarter_rows * wslice),
        name="merge",
    )(own_sums, swapped)
    came[0], *merged = lax.optimization_barrier((came[0], *merged))
    both = jax.ShapeDtypeStruct((groups // 2,) + piece.shape, BF16)
    keep, send = pl.pallas_call(
        functools.partial(route_kernel, groups),
        out_shape=[both] * 2,
        in_specs=[spec(VMEM)] * groups,
        out_specs=[spec(VMEM)] * 2,
        scratch_shapes=[VMEM((groups,) + piece.shape, BF16)],
        compiler_params=params(8),
        cost_estimate=cost(0, 8 * groups * half_rows * wslice),
        name="route",
    )(*came)
    near = lift(send, 1)
    merged = [merged[0]] + [swap(merged[p], p) for p in range(1, groups)]
    direct = pl.pallas_call(
        functools.partial(direct_kernel, groups),
        out_shape=[small] * groups,
        in_specs=[spec(VMEM)] * groups,
        out_specs=[spec(VMEM)] * groups,
        scratch_shapes=[VMEM((groups,) + small.shape, BF16)],
        compiler_params=params(8),
        cost_estimate=cost(0, 8 * groups * quarter_rows * wslice),
        name="direct",
    )(*merged)
    sums = pl.pallas_call(
        functools.partial(add_kernel, groups),
        out_shape=[piece] * (groups // 2 - 1),
        in_specs=[spec(VMEM)] * 2,
        out_specs=[spec(VMEM)] * (groups // 2 - 1),
        compiler_params=params(8),
        cost_estimate=cost(groups * half_rows * wslice, 6 * groups * half_rows * wslice),
        name="add",
    )(keep, near)
    moved = [keep, near] + [lift(sums[m // 2 - 1], m) for m in range(2, groups, 2)]
    moved += [direct[0]] + [lift(direct[m], m) for m in range(1, groups)]

    rebuilt = pl.pallas_call(
        functools.partial(finish_kernel, groups),
        out_shape=jax.ShapeDtypeStruct((tok_rows, 2 * wslice), BF16),
        in_specs=[spec(VMEM)] * (len(moved) + 1),
        out_specs=spec(VMEM),
        compiler_params=params(8),
        cost_estimate=cost(0, 4 * (groups + 1) * tok_rows * wslice),
        name="finish",
    )(*moved, bias_rows)
    return (code_values, rebuilt)


def solution(mesh):
    in_specs = (
        P("tok", None),
        P(),
        P("tok", "feat"),
        P("feat"),
        P("feat", "tok"),
        P(None, "feat", None),
        P(None, "feat"),
    )
    out_specs = (P("tok", "feat"), P("tok", "feat"))
    return jax.shard_map(
        on_device, mesh=mesh, in_specs=in_specs, out_specs=out_specs, check_vma=False
    )
```

```python
import functools

import jax
import jax.numpy as jnp
from jax import lax
from jax.experimental import pallas as pl
from jax.experimental.pallas import tpu as pltpu
from jax.sharding import PartitionSpec as P

BLOCK = 64
SLOTS = 4
LANES = 128
ACTIVE = SLOTS * BLOCK
VMEM = pltpu.VMEM
SMEM = pltpu.SMEM
HBM = pltpu.HBM
BF16 = jnp.bfloat16
F32 = jnp.float32


def spec(space):
    return pl.BlockSpec(memory_space=space)


def params(mib):
    return pltpu.CompilerParams(vmem_limit_bytes=mib << 20)


def cost(flops, nbytes):
    return pl.CostEstimate(flops=flops, bytes_accessed=nbytes, transcendentals=0)


def pin(value):
    return pltpu.with_memory_space_constraint(value, HBM)


def place():
    tok = lax.axis_index("tok")
    return lax.axis_index("feat"), tok >> 1, tok & 1


def split_kernel(groups, tok_ref, *outs):
    _, c, k = place()
    wslice = outs[0].shape[2]
    for p in range(groups):
        for half in range(2):
            u = ((c ^ p) << 1) + (k ^ half)
            cols = pl.ds(pl.multiple_of(u * wslice, wslice), wslice)
            outs[p][half] = tok_ref[:, cols]


def pick_pair(first, second, odd_first, odd_second):
    low = lax.broadcasted_iota(jnp.int32, first.shape, 1) < BLOCK
    a = jnp.where(odd_first, pltpu.roll(first, BLOCK, 1), first)
    b = jnp.where(odd_second, second, pltpu.roll(second, BLOCK, 1))
    return jnp.where(low, a, b)


def columns_kernel(groups, ids_ref, w_ref, out_ref):
    _, c, k = place()
    for p in range(groups):
        tile = ((c ^ p) << 1) + k
        for pair in range(SLOTS // 2):
            windows = []
            odds = []
            for slot in (2 * pair, 2 * pair + 1):
                block = ids_ref[tile, slot]
                start = pl.multiple_of((block >> 1) * LANES, LANES)
                windows.append(w_ref[:, pl.ds(start, LANES)])
                odds.append((block & 1) == 1)
            picked = pick_pair(windows[0].astype(F32), windows[1].astype(F32), *odds)
            out_ref[p, :, pair * LANES : (pair + 1) * LANES] = picked.astype(BF16)


def stage_kernel(src, dst, sems):
    parts = sems.shape[0]
    height = src.shape[0] // parts
    copies = []
    for i in range(parts):
        some = pl.ds(i * height, height)
        copy = pltpu.make_async_copy(src.at[some, :], dst.at[some, :], sems.at[i])
        copy.start()
        copies.append(copy)
    for copy in copies:
        copy.wait()


def encode_kernel(groups, *refs):
    bias_ref, pieces, (own_ref, oth_ref, out_ref) = refs[0], refs[1 : 1 + groups], refs[1 + groups :]
    _, c, k = place()
    bias = [bias_ref[pl.ds(2 * c + (k ^ half), 1), :] for half in range(2)]
    for p in range(groups):
        mine, other = [
            (pieces[p][half].astype(F32) - bias[half]).astype(BF16) for half in range(2)
        ]
        acc = jnp.dot(mine, own_ref[p], preferred_element_type=F32)
        acc += jnp.dot(other, oth_ref[p], preferred_element_type=F32)
        out_ref[p] = acc.astype(BF16)


def decode_kernel(groups, *refs):
    ids_ref, counts_ref, bias_ref = refs[:3]
    parts = refs[3 : 3 + groups]
    own_ref, oth_ref, code_ref = refs[3 + groups : 6 + groups]
    firsts = refs[6 + groups : 6 + 2 * groups]
    keep_ref, send_ref = refs[6 + 2 * groups :]
    f, c, k = place()
    even = (f & 1) == 0
    lane = lax.broadcasted_iota(jnp.int32, (1, LANES), 1)
    for p in range(groups):
        tile = ((c ^ p) << 1) + k
        count = counts_ref[tile]
        code = []
        listed = []
        for pair in range(SLOTS // 2):
            cols = slice(pair * LANES, (pair + 1) * LANES)
            pre = parts[0][p, :, cols].astype(F32)
            for q in range(1, groups):
                pre += parts[q][p ^ q, :, cols].astype(F32)
            bias = []
            odds = []
            for slot in (2 * pair, 2 * pair + 1):
                block = ids_ref[tile, slot]
                listed.append(pl.ds(pl.multiple_of(block * BLOCK, BLOCK), BLOCK))
                bias.append(bias_ref[pl.ds(block >> 1, 1), :])
                odds.append((block & 1) == 1)
            row = pick_pair(bias[0], bias[1], *odds)
            live = (lane >= BLOCK).astype(jnp.int32) + 2 * pair < count
            value = jnp.where(live, jnp.maximum(pre + row, 0.0), 0.0).astype(BF16)
            code.append(value)
        code = jnp.concatenate(code, axis=1)
        if p == 0:
            code_ref[...] = code
        height = code.shape[0] // 4
        for half, ref in ((k, own_ref), (1 - k, oth_ref)):
            rows = jnp.concatenate([ref[some, :] for some in listed], axis=0)
            result = jnp.dot(code, rows, preferred_element_type=F32).astype(BF16)
            firsts[p][half] = result[: 2 * height]
            third, fourth = result[2 * height : 3 * height], result[3 * height :]
            keep_ref[p, half] = jnp.where(even, third, fourth)
            send_ref[p, half] = jnp.where(even, fourth, third)


def route_kernel(groups, *refs):
    came, (keep_ref, send_ref, held) = refs[:groups], refs[groups:]
    f, c, _ = place()
    for p in range(groups):
        held[p] = came[p][...]
    for m in range(0, groups, 2):
        keep_ref[m // 2] = held[c ^ f ^ m]
        send_ref[m // 2] = held[c ^ f ^ m ^ 1]


def add_kernel(groups, *refs):
    keep_ref, came_ref, *rest = refs
    straight, outs = rest[: groups // 2 - 1], rest[groups // 2 - 1 :]
    for i in range(1, groups // 2):
        total = keep_ref[i].astype(F32) + came_ref[i].astype(F32)
        rows = total.shape[1]
        outs[i - 1][:, :rows] = total.astype(BF16)
        outs[i - 1][:, rows:] = straight[i - 1][...]


def merge_kernel(groups, keep_ref, came_ref, *outs):
    for p in range(groups):
        outs[p][...] = (keep_ref[p].astype(F32) + came_ref[p].astype(F32)).astype(BF16)


def direct_kernel(groups, *refs):
    came, outs, held = refs[:groups], refs[groups : 2 * groups], refs[2 * groups]
    f, c, _ = place()
    for p in range(groups):
        held[p] = came[p][...]
    for m in range(groups):
        outs[m][...] = held[c ^ f ^ m]


def finish_kernel(groups, *refs):
    keep_ref, came_ref, mine_ref, *rest = refs[:-2]
    bias_ref, out_ref = refs[-2:]
    far, odd = rest[: groups // 2 - 1], rest[groups // 2 - 1 :]
    f, _, _ = place()
    _, rows, wslice = mine_ref.shape
    for half in range(2):
        cols = slice(half * wslice, (half + 1) * wslice)
        bias = bias_ref[pl.ds(2 * f + half, 1), :]
        first = keep_ref[0, half].astype(F32) + came_ref[0, half].astype(F32)
        same = mine_ref[half].astype(F32)
        for ref in far:
            first += ref[half, : 2 * rows].astype(F32)
            same += ref[half, 2 * rows :].astype(F32)
        out_ref[: 2 * rows, cols] = (first + bias).astype(BF16)
        other = odd[0][half].astype(F32)
        for ref in odd[1:]:
            other += ref[half].astype(F32)
        for total, parity in ((same, f & 1), (other, 1 - (f & 1))):
            start = pl.multiple_of(2 * rows + parity * rows, rows)
            out_ref[pl.ds(start, rows), cols] = (total + bias).astype(BF16)


def on_device(tokens, dec_bias, enc_weight, enc_bias, dec_weight, block_ids, block_counts):
    tile_count = lax.axis_size("tok")
    groups = lax.axis_size("feat")
    tok_rows, width = tokens.shape
    wslice = width // tile_count
    feats = enc_weight.shape[1]
    ids = block_ids[:, 0, :]
    counts = block_counts[:, 0]
    bias_rows = dec_bias.astype(F32).reshape(tile_count, wslice)
    enc_bias_rows = enc_bias.astype(F32).reshape(feats // LANES, LANES)

    def swap(value, p):
        pairs = [(i, i ^ (2 * p)) for i in range(tile_count)]
        return lax.ppermute(value, "tok", pairs)

    def lift(value, m):
        return lax.ppermute(value, "feat", [(i, i ^ m) for i in range(groups)])

    cores = [(i, i ^ 1) for i in range(tile_count)]
    enc_other = lax.ppermute(enc_weight, "tok", cores)
    dec_other = lax.ppermute(dec_weight, "tok", cores)

    sent = pl.pallas_call(
        functools.partial(split_kernel, groups),
        out_shape=[jax.ShapeDtypeStruct((2, tok_rows, wslice), BF16)] * groups,
        in_specs=[spec(VMEM)],
        out_specs=[spec(VMEM)] * groups,
        compiler_params=params(8),
        cost_estimate=cost(0, 4 * width * tok_rows),
        name="split",
    )(tokens)
    pieces = [sent[0]] + [swap(sent[p], p) for p in range(1, groups)]

    chunk = min(wslice, 256)

    def columns(weight):
        return pl.pallas_call(
            functools.partial(columns_kernel, groups),
            out_shape=jax.ShapeDtypeStruct((groups, wslice, ACTIVE), BF16),
            grid=(wslice // chunk,),
            in_specs=[spec(SMEM), pl.BlockSpec((chunk, feats), lambda i: (i, 0))],
            out_specs=pl.BlockSpec((groups, chunk, ACTIVE), lambda i: (0, i, 0)),
            compiler_params=params(8),
            cost_estimate=cost(0, 2 * wslice * (feats + groups * ACTIVE)),
            name="columns",
        )(ids, weight)

    own_cols = columns(enc_weight)
    oth_cols = columns(enc_other)
    flops = 4 * groups * tok_rows * wslice * ACTIVE
    part = pl.pallas_call(
        functools.partial(encode_kernel, groups),
        out_shape=jax.ShapeDtypeStruct((groups, tok_rows, ACTIVE), BF16),
        in_specs=[spec(VMEM)] * (groups + 3),
        out_specs=spec(VMEM),
        compiler_params=params(8),
        cost_estimate=cost(flops, 4 * groups * wslice * ACTIVE),
        name="encode",
    )(bias_rows, *pieces, own_cols, oth_cols)
    parts = [part] + [swap(part, p) for p in range(1, groups)]

    dec_staged = pl.pallas_call(
        stage_kernel,
        out_shape=jax.ShapeDtypeStruct(dec_weight.shape, BF16),
        in_specs=[spec(pl.ANY)],
        out_specs=spec(VMEM),
        scratch_shapes=[pltpu.SemaphoreType.DMA((8,))],
        compiler_params=params(8),
        cost_estimate=cost(0, 4 * wslice * feats),
        name="stage",
    )(dec_other)
    half_rows = tok_rows // 2
    quarter_rows = tok_rows // 4
    piece = jax.ShapeDtypeStruct((2, half_rows, wslice), BF16)
    small = jax.ShapeDtypeStruct((2, quarter_rows, wslice), BF16)
    smalls = jax.ShapeDtypeStruct((groups, 2, quarter_rows, wslice), BF16)
    code_values, *outgoing = pl.pallas_call(
        functools.partial(decode_kernel, groups),
        out_shape=[jax.ShapeDtypeStruct((tok_rows, ACTIVE), BF16)]
        + [piece] * groups
        + [smalls] * 2,
        in_specs=[spec(SMEM)] * 2 + [spec(VMEM)] * (3 + groups),
        out_specs=[spec(VMEM)] * (3 + groups),
        compiler_params=params(8),
        cost_estimate=cost(flops, 4 * groups * wslice * ACTIVE),
        name="decode",
    )(ids, counts, enc_bias_rows, *parts, dec_weight, dec_staged)
    firsts, (own_sums, sent_sums) = outgoing[:groups], outgoing[groups:]

    swapped = lift(sent_sums, 1)
    came = [firsts[0]] + [swap(firsts[p], p) for p in range(1, groups)]
    merged = pl.pallas_call(
        functools.partial(merge_kernel, groups),
        out_shape=[small] * groups,
        in_specs=[spec(VMEM)] * 2,
        out_specs=[spec(VMEM)] * groups,
        compiler_params=params(8),
        cost_estimate=cost(0, 8 * groups * quarter_rows * wslice),
        name="merge",
    )(own_sums, swapped)
    came[0], *merged = lax.optimization_barrier((came[0], *merged))
    both = jax.ShapeDtypeStruct((groups // 2,) + piece.shape, BF16)
    keep, send = pl.pallas_call(
        functools.partial(route_kernel, groups),
        out_shape=[both] * 2,
        in_specs=[spec(VMEM)] * groups,
        out_specs=[spec(VMEM)] * 2,
        scratch_shapes=[VMEM((groups,) + piece.shape, BF16)],
        compiler_params=params(8),
        cost_estimate=cost(0, 8 * groups * half_rows * wslice),
        name="route",
    )(*came)
    near = lift(send, 1)
    merged = [merged[0]] + [swap(merged[p], p) for p in range(1, groups)]
    direct = pl.pallas_call(
        functools.partial(direct_kernel, groups),
        out_shape=[small] * groups,
        in_specs=[spec(VMEM)] * groups,
        out_specs=[spec(VMEM)] * groups,
        scratch_shapes=[VMEM((groups,) + small.shape, BF16)],
        compiler_params=params(8),
        cost_estimate=cost(0, 8 * groups * quarter_rows * wslice),
        name="direct",
    )(*merged)
    far = jax.ShapeDtypeStruct((2, half_rows + quarter_rows, wslice), BF16)
    sums = pl.pallas_call(
        functools.partial(add_kernel, groups),
        out_shape=[far] * (groups // 2 - 1),
        in_specs=[spec(VMEM)] * (1 + groups // 2),
        out_specs=[spec(VMEM)] * (groups // 2 - 1),
        compiler_params=params(8),
        cost_estimate=cost(groups * half_rows * wslice, 6 * groups * half_rows * wslice),
        name="add",
    )(keep, near, *direct[2::2])
    moved = [keep, near, direct[0]]
    moved += [lift(sums[m // 2 - 1], m) for m in range(2, groups, 2)]
    moved += [lift(direct[m], m) for m in range(1, groups, 2)]

    rebuilt = pl.pallas_call(
        functools.partial(finish_kernel, groups),
        out_shape=jax.ShapeDtypeStruct((tok_rows, 2 * wslice), BF16),
        in_specs=[spec(VMEM)] * (len(moved) + 1),
        out_specs=spec(VMEM),
        compiler_params=params(8),
        cost_estimate=cost(0, 4 * (groups + 1) * tok_rows * wslice),
        name="finish",
    )(*moved, bias_rows)
    return (code_values, rebuilt)


def solution(mesh):
    in_specs = (
        P("tok", None),
        P(),
        P("tok", "feat"),
        P("feat"),
        P("feat", "tok"),
        P(None, "feat", None),
        P(None, "feat"),
    )
    out_specs = (P("tok", "feat"), P("tok", "feat"))
    return jax.shard_map(
        on_device, mesh=mesh, in_specs=in_specs, out_specs=out_specs, check_vma=False
    )
```

```python
import functools

import jax
import jax.numpy as jnp
from jax import lax
from jax.experimental import pallas as pl
from jax.experimental.pallas import tpu as pltpu
from jax.sharding import PartitionSpec as P

BLOCK = 64
SLOTS = 4
LANES = 128
ACTIVE = SLOTS * BLOCK
VMEM = pltpu.VMEM
SMEM = pltpu.SMEM
HBM = pltpu.HBM
BF16 = jnp.bfloat16
F32 = jnp.float32


def spec(space):
    return pl.BlockSpec(memory_space=space)


def params(mib):
    return pltpu.CompilerParams(vmem_limit_bytes=mib << 20)


def cost(flops, nbytes):
    return pl.CostEstimate(flops=flops, bytes_accessed=nbytes, transcendentals=0)


def pin(value):
    return pltpu.with_memory_space_constraint(value, HBM)


def place():
    tok = lax.axis_index("tok")
    return lax.axis_index("feat"), tok >> 1, tok & 1


def split_kernel(groups, tok_ref, *outs):
    _, c, k = place()
    wslice = outs[0].shape[2]
    for p in range(groups):
        for half in range(2):
            u = ((c ^ p) << 1) + (k ^ half)
            cols = pl.ds(pl.multiple_of(u * wslice, wslice), wslice)
            outs[p][half] = tok_ref[:, cols]


def pick_pair(first, second, odd_first, odd_second):
    low = lax.broadcasted_iota(jnp.int32, first.shape, 1) < BLOCK
    a = jnp.where(odd_first, pltpu.roll(first, BLOCK, 1), first)
    b = jnp.where(odd_second, second, pltpu.roll(second, BLOCK, 1))
    return jnp.where(low, a, b)


def columns_kernel(groups, ids_ref, w_ref, out_ref):
    _, c, k = place()
    low = lax.broadcasted_iota(jnp.int32, (w_ref.shape[0], LANES), 1) < BLOCK
    for p in range(groups):
        tile = ((c ^ p) << 1) + k
        for pair in range(SLOTS // 2):
            halves = []
            for slot in range(2):
                block = ids_ref[tile, 2 * pair + slot]
                start = pl.multiple_of((block >> 1) * LANES, LANES)
                turn = ((block & 1) ^ slot) * BLOCK
                halves.append(pltpu.roll(w_ref[:, pl.ds(start, LANES)], turn, 1))
            out_ref[p, :, pair * LANES : (pair + 1) * LANES] = jnp.where(low, *halves)


def stage_kernel(src, dst, sems):
    parts = sems.shape[0]
    height = src.shape[0] // parts
    copies = []
    for i in range(parts):
        some = pl.ds(i * height, height)
        copy = pltpu.make_async_copy(src.at[some, :], dst.at[some, :], sems.at[i])
        copy.start()
        copies.append(copy)
    for copy in copies:
        copy.wait()


def encode_kernel(groups, low, *refs):
    bias_ref, own_ref, oth_ref = refs[:3]
    done, pieces, out_ref = refs[3 : 3 + bool(low)], refs[3 + bool(low) : -1], refs[-1]
    _, c, k = place()
    for ref in done:
        out_ref[:low] = ref[...]
    wslice = own_ref.shape[1]
    bias = [bias_ref[pl.ds(2 * c + (k ^ half), 1), :] for half in range(2)]
    for p, ref in enumerate(pieces, low):
        mine, other = [
            (ref[half].astype(F32) - bias[half]).astype(BF16) for half in range(2)
        ]
        acc = jnp.dot(mine, own_ref[p], preferred_element_type=F32)
        acc += jnp.dot(other, oth_ref[p], preferred_element_type=F32)
        out_ref[p] = acc.astype(BF16)


def decode_kernel(groups, *refs):
    ids_ref, counts_ref, bias_ref = refs[:3]
    parts = refs[3 : 3 + groups]
    own_ref, oth_ref, code_ref = refs[3 + groups : 6 + groups]
    firsts = refs[6 + groups : 6 + 2 * groups]
    keep_ref, send_ref = refs[6 + 2 * groups :]
    f, c, k = place()
    even = (f & 1) == 0
    lane = lax.broadcasted_iota(jnp.int32, (1, LANES), 1)
    for p in range(groups):
        tile = ((c ^ p) << 1) + k
        count = counts_ref[tile]
        code = []
        listed = []
        for pair in range(SLOTS // 2):
            cols = slice(pair * LANES, (pair + 1) * LANES)
            pre = parts[0][p, :, cols].astype(F32)
            for q in range(1, groups):
                pre += parts[q][p ^ q, :, cols].astype(F32)
            bias = []
            odds = []
            for slot in (2 * pair, 2 * pair + 1):
                block = ids_ref[tile, slot]
                listed.append(pl.ds(pl.multiple_of(block * BLOCK, BLOCK), BLOCK))
                bias.append(bias_ref[pl.ds(block >> 1, 1), :])
                odds.append((block & 1) == 1)
            row = pick_pair(bias[0], bias[1], *odds)
            live = (lane >= BLOCK).astype(jnp.int32) + 2 * pair < count
            value = jnp.where(live, jnp.maximum(pre + row, 0.0), 0.0).astype(BF16)
            code.append(value)
        code = jnp.concatenate(code, axis=1)
        if p == 0:
            code_ref[...] = code
        height = code.shape[0] // 4
        for half, ref in ((k, own_ref), (1 - k, oth_ref)):
            rows = jnp.concatenate([ref[some, :] for some in listed], axis=0)
            result = jnp.dot(code, rows, preferred_element_type=F32).astype(BF16)
            firsts[p][half] = result[: 2 * height]
            third, fourth = result[2 * height : 3 * height], result[3 * height :]
            keep_ref[p, half] = jnp.where(even, third, fourth)
            send_ref[p, half] = jnp.where(even, fourth, third)


def route_kernel(groups, *refs):
    came, (keep_ref, send_ref, held) = refs[:groups], refs[groups:]
    f, c, _ = place()
    for p in range(groups):
        held[p] = came[p][...]
    for m in range(0, groups, 2):
        keep_ref[m // 2] = held[c ^ f ^ m]
        send_ref[m // 2] = held[c ^ f ^ m ^ 1]


def add_kernel(groups, *refs):
    keep_ref, came_ref, *rest = refs
    straight, outs = rest[: groups // 2 - 1], rest[groups // 2 - 1 :]
    for i in range(1, groups // 2):
        total = keep_ref[i].astype(F32) + came_ref[i].astype(F32)
        rows = total.shape[1]
        outs[i - 1][:, :rows] = total.astype(BF16)
        outs[i - 1][:, rows:] = straight[i - 1][...]


def merge_kernel(groups, keep_ref, came_ref, *outs):
    for p in range(groups):
        outs[p][...] = (keep_ref[p].astype(F32) + came_ref[p].astype(F32)).astype(BF16)


def direct_kernel(groups, *refs):
    came, outs, held = refs[:groups], refs[groups : 2 * groups], refs[2 * groups]
    f, c, _ = place()
    for p in range(groups):
        held[p] = came[p][...]
    for m in range(groups):
        outs[m][...] = held[c ^ f ^ m]


def finish_kernel(groups, *refs):
    keep_ref, came_ref, mine_ref, *rest = refs[:-2]
    bias_ref, out_ref = refs[-2:]
    far, odd = rest[: groups // 2 - 1], rest[groups // 2 - 1 :]
    f, _, _ = place()
    _, rows, wslice = mine_ref.shape
    for half in range(2):
        cols = slice(half * wslice, (half + 1) * wslice)
        bias = bias_ref[pl.ds(2 * f + half, 1), :]
        first = keep_ref[0, half].astype(F32) + came_ref[0, half].astype(F32)
        same = mine_ref[half].astype(F32)
        for ref in far:
            first += ref[half, : 2 * rows].astype(F32)
            same += ref[half, 2 * rows :].astype(F32)
        out_ref[: 2 * rows, cols] = (first + bias).astype(BF16)
        other = odd[0][half].astype(F32)
        for ref in odd[1:]:
            other += ref[half].astype(F32)
        for total, parity in ((same, f & 1), (other, 1 - (f & 1))):
            start = pl.multiple_of(2 * rows + parity * rows, rows)
            out_ref[pl.ds(start, rows), cols] = (total + bias).astype(BF16)


def on_device(tokens, dec_bias, enc_weight, enc_bias, dec_weight, block_ids, block_counts):
    tile_count = lax.axis_size("tok")
    groups = lax.axis_size("feat")
    tok_rows, width = tokens.shape
    wslice = width // tile_count
    feats = enc_weight.shape[1]
    ids = block_ids[:, 0, :]
    counts = block_counts[:, 0]
    bias_rows = dec_bias.astype(F32).reshape(tile_count, wslice)
    enc_bias_rows = enc_bias.astype(F32).reshape(feats // LANES, LANES)

    def swap(value, p):
        pairs = [(i, i ^ (2 * p)) for i in range(tile_count)]
        return lax.ppermute(value, "tok", pairs)

    def lift(value, m):
        return lax.ppermute(value, "feat", [(i, i ^ m) for i in range(groups)])

    cores = [(i, i ^ 1) for i in range(tile_count)]
    enc_other = lax.ppermute(enc_weight, "tok", cores)
    dec_other = lax.ppermute(dec_weight, "tok", cores)

    sent = pl.pallas_call(
        functools.partial(split_kernel, groups),
        out_shape=[jax.ShapeDtypeStruct((2, tok_rows, wslice), BF16)] * groups,
        in_specs=[spec(VMEM)],
        out_specs=[spec(VMEM)] * groups,
        compiler_params=params(8),
        cost_estimate=cost(0, 4 * width * tok_rows),
        name="split",
    )(tokens)
    pieces = [sent[0]] + [swap(sent[p], p) for p in range(1, groups)]

    def columns(weight):
        return pl.pallas_call(
            functools.partial(columns_kernel, groups),
            out_shape=jax.ShapeDtypeStruct((groups, wslice, ACTIVE), BF16),
            in_specs=[spec(SMEM), spec(VMEM)],
            out_specs=spec(VMEM),
            compiler_params=params(8),
            cost_estimate=cost(0, 2 * wslice * (feats + groups * ACTIVE)),
            name="columns",
        )(ids, weight)

    own_cols = columns(enc_weight)
    oth_cols = columns(enc_other)
    flops = 4 * groups * tok_rows * wslice * ACTIVE
    part = []
    for low, high in ((0, groups // 2), (groups // 2, groups)):
        part = [
            pl.pallas_call(
                functools.partial(encode_kernel, groups, low),
                out_shape=jax.ShapeDtypeStruct((high, tok_rows, ACTIVE), BF16),
                in_specs=[spec(VMEM)] * (3 + len(part) + high - low),
                out_specs=spec(VMEM),
                compiler_params=params(8),
                cost_estimate=cost(flops // 2, 2 * groups * wslice * ACTIVE),
                name="encode",
            )(bias_rows, own_cols, oth_cols, *part, *pieces[low:high])
        ]
    part = part[0]
    parts = [part] + [swap(part, p) for p in range(1, groups)]

    dec_staged = pl.pallas_call(
        stage_kernel,
        out_shape=jax.ShapeDtypeStruct(dec_weight.shape, BF16),
        in_specs=[spec(pl.ANY)],
        out_specs=spec(VMEM),
        scratch_shapes=[pltpu.SemaphoreType.DMA((8,))],
        compiler_params=params(8),
        cost_estimate=cost(0, 4 * wslice * feats),
        name="stage",
    )(dec_other)
    half_rows = tok_rows // 2
    quarter_rows = tok_rows // 4
    piece = jax.ShapeDtypeStruct((2, half_rows, wslice), BF16)
    small = jax.ShapeDtypeStruct((2, quarter_rows, wslice), BF16)
    smalls = jax.ShapeDtypeStruct((groups, 2, quarter_rows, wslice), BF16)
    code_values, *outgoing = pl.pallas_call(
        functools.partial(decode_kernel, groups),
        out_shape=[jax.ShapeDtypeStruct((tok_rows, ACTIVE), BF16)]
        + [piece] * groups
        + [smalls] * 2,
        in_specs=[spec(SMEM)] * 2 + [spec(VMEM)] * (3 + groups),
        out_specs=[spec(VMEM)] * (3 + groups),
        compiler_params=params(8),
        cost_estimate=cost(flops, 4 * groups * wslice * ACTIVE),
        name="decode",
    )(ids, counts, enc_bias_rows, *parts, dec_weight, dec_staged)
    firsts, (own_sums, sent_sums) = outgoing[:groups], outgoing[groups:]

    swapped = lift(sent_sums, 1)
    came = [firsts[0]] + [swap(firsts[p], p) for p in range(1, groups)]
    merged = pl.pallas_call(
        functools.partial(merge_kernel, groups),
        out_shape=[small] * groups,
        in_specs=[spec(VMEM)] * 2,
        out_specs=[spec(VMEM)] * groups,
        compiler_params=params(8),
        cost_estimate=cost(0, 8 * groups * quarter_rows * wslice),
        name="merge",
    )(own_sums, swapped)
    came[0], *merged = lax.optimization_barrier((came[0], *merged))
    both = jax.ShapeDtypeStruct((groups // 2,) + piece.shape, BF16)
    keep, send = pl.pallas_call(
        functools.partial(route_kernel, groups),
        out_shape=[both] * 2,
        in_specs=[spec(VMEM)] * groups,
        out_specs=[spec(VMEM)] * 2,
        scratch_shapes=[VMEM((groups,) + piece.shape, BF16)],
        compiler_params=params(8),
        cost_estimate=cost(0, 8 * groups * half_rows * wslice),
        name="route",
    )(*came)
    near = lift(send, 1)
    merged = [merged[0]] + [swap(merged[p], p) for p in range(1, groups)]
    direct = pl.pallas_call(
        functools.partial(direct_kernel, groups),
        out_shape=[small] * groups,
        in_specs=[spec(VMEM)] * groups,
        out_specs=[spec(VMEM)] * groups,
        scratch_shapes=[VMEM((groups,) + small.shape, BF16)],
        compiler_params=params(8),
        cost_estimate=cost(0, 8 * groups * quarter_rows * wslice),
        name="direct",
    )(*merged)
    far = jax.ShapeDtypeStruct((2, half_rows + quarter_rows, wslice), BF16)
    sums = pl.pallas_call(
        functools.partial(add_kernel, groups),
        out_shape=[far] * (groups // 2 - 1),
        in_specs=[spec(VMEM)] * (1 + groups // 2),
        out_specs=[spec(VMEM)] * (groups // 2 - 1),
        compiler_params=params(8),
        cost_estimate=cost(groups * half_rows * wslice, 6 * groups * half_rows * wslice),
        name="add",
    )(keep, near, *direct[2::2])
    moved = [keep, near, direct[0]]
    moved += [lift(sums[m // 2 - 1], m) for m in range(2, groups, 2)]
    moved += [lift(direct[m], m) for m in range(1, groups, 2)]

    rebuilt = pl.pallas_call(
        functools.partial(finish_kernel, groups),
        out_shape=jax.ShapeDtypeStruct((tok_rows, 2 * wslice), BF16),
        in_specs=[spec(VMEM)] * (len(moved) + 1),
        out_specs=spec(VMEM),
        compiler_params=params(8),
        cost_estimate=cost(0, 4 * (groups + 1) * tok_rows * wslice),
        name="finish",
    )(*moved, bias_rows)
    return (code_values, rebuilt)


def solution(mesh):
    in_specs = (
        P("tok", None),
        P(),
        P("tok", "feat"),
        P("feat"),
        P("feat", "tok"),
        P(None, "feat", None),
        P(None, "feat"),
    )
    out_specs = (P("tok", "feat"), P("tok", "feat"))
    return jax.shard_map(
        on_device, mesh=mesh, in_specs=in_specs, out_specs=out_specs, check_vma=False
    )
```

```python
import functools

import jax
import jax.numpy as jnp
from jax import lax
from jax.experimental import pallas as pl
from jax.experimental.pallas import tpu as pltpu
from jax.sharding import PartitionSpec as P

BLOCK = 64
SLOTS = 4
LANES = 128
ACTIVE = SLOTS * BLOCK
VMEM = pltpu.VMEM
SMEM = pltpu.SMEM
HBM = pltpu.HBM
BF16 = jnp.bfloat16
F32 = jnp.float32


def spec(space):
    return pl.BlockSpec(memory_space=space)


def params(mib):
    return pltpu.CompilerParams(vmem_limit_bytes=mib << 20)


def cost(flops, nbytes):
    return pl.CostEstimate(flops=flops, bytes_accessed=nbytes, transcendentals=0)


def pin(value):
    return pltpu.with_memory_space_constraint(value, HBM)


def place():
    tok = lax.axis_index("tok")
    return lax.axis_index("feat"), tok >> 1, tok & 1


def split_kernel(groups, tok_ref, bias_ref, *refs):
    outs, (held, bias, sems) = refs[:groups], refs[groups:]
    _, c, k = place()
    wslice = outs[0].shape[2]
    parts = sems.shape[0] - 1
    height = held.shape[0] // parts
    copies = [pltpu.make_async_copy(bias_ref, bias, sems.at[parts])]
    for i in range(parts):
        some = pl.ds(i * height, height)
        copies.append(pltpu.make_async_copy(tok_ref.at[some, :], held.at[some, :], sems.at[i]))
    for copy in copies:
        copy.start()
    for copy in copies:
        copy.wait()
    for p in range(groups):
        for half in range(2):
            u = ((c ^ p) << 1) + (k ^ half)
            cols = pl.ds(pl.multiple_of(u * wslice, wslice), wslice)
            value = held[:, cols].astype(F32) - bias[cols].astype(F32)[None, :]
            outs[p][half] = value.astype(BF16)


def pick_pair(first, second, odd_first, odd_second):
    low = lax.broadcasted_iota(jnp.int32, first.shape, 1) < BLOCK
    a = jnp.where(odd_first, pltpu.roll(first, BLOCK, 1), first)
    b = jnp.where(odd_second, second, pltpu.roll(second, BLOCK, 1))
    return jnp.where(low, a, b)


def columns_kernel(groups, ids_ref, w_ref, out_ref):
    _, c, k = place()
    low = lax.broadcasted_iota(jnp.int32, (w_ref.shape[0], LANES), 1) < BLOCK
    for p in range(groups):
        tile = ((c ^ p) << 1) + k
        for pair in range(SLOTS // 2):
            halves = []
            for slot in range(2):
                block = ids_ref[tile, 2 * pair + slot]
                start = pl.multiple_of((block >> 1) * LANES, LANES)
                turn = ((block & 1) ^ slot) * BLOCK
                halves.append(pltpu.roll(w_ref[:, pl.ds(start, LANES)], turn, 1))
            out_ref[p, :, pair * LANES : (pair + 1) * LANES] = jnp.where(low, *halves)


def stage_kernel(src, dst, sems):
    parts = sems.shape[0]
    height = src.shape[0] // parts
    copies = []
    for i in range(parts):
        some = pl.ds(i * height, height)
        copy = pltpu.make_async_copy(src.at[some, :], dst.at[some, :], sems.at[i])
        copy.start()
        copies.append(copy)
    for copy in copies:
        copy.wait()


def encode_kernel(groups, low, *refs):
    own_ref, oth_ref = refs[:2]
    done, pieces, out_ref = refs[2 : 2 + bool(low)], refs[2 + bool(low) : -1], refs[-1]
    for ref in done:
        out_ref[:low] = ref[...]
    for p, ref in enumerate(pieces, low):
        acc = jnp.dot(ref[0], own_ref[p], preferred_element_type=F32)
        acc += jnp.dot(ref[1], oth_ref[p], preferred_element_type=F32)
        out_ref[p] = acc.astype(BF16)


def decode_kernel(groups, *refs):
    ids_ref, counts_ref, bias_ref = refs[:3]
    parts = refs[3 : 3 + groups]
    own_ref, oth_ref, code_ref = refs[3 + groups : 6 + groups]
    firsts = refs[6 + groups : 6 + 2 * groups]
    keep_ref, send_ref = refs[6 + 2 * groups :]
    f, c, k = place()
    even = (f & 1) == 0
    lane = lax.broadcasted_iota(jnp.int32, (1, LANES), 1)
    for p in range(groups):
        tile = ((c ^ p) << 1) + k
        count = counts_ref[tile]
        code = []
        listed = []
        for pair in range(SLOTS // 2):
            cols = slice(pair * LANES, (pair + 1) * LANES)
            pre = parts[0][p, :, cols].astype(F32)
            for q in range(1, groups):
                pre += parts[q][p ^ q, :, cols].astype(F32)
            bias = []
            odds = []
            for slot in (2 * pair, 2 * pair + 1):
                block = ids_ref[tile, slot]
                listed.append(pl.ds(pl.multiple_of(block * BLOCK, BLOCK), BLOCK))
                bias.append(bias_ref[pl.ds(block >> 1, 1), :])
                odds.append((block & 1) == 1)
            row = pick_pair(bias[0], bias[1], *odds)
            live = (lane >= BLOCK).astype(jnp.int32) + 2 * pair < count
            value = jnp.where(live, jnp.maximum(pre + row, 0.0), 0.0).astype(BF16)
            code.append(value)
        code = jnp.concatenate(code, axis=1)
        if p == 0:
            code_ref[...] = code
        height = code.shape[0] // 4
        for half, ref in ((k, own_ref), (1 - k, oth_ref)):
            rows = jnp.concatenate([ref[some, :] for some in listed], axis=0)
            result = jnp.dot(code, rows, preferred_element_type=F32).astype(BF16)
            firsts[p][half] = result[: 2 * height]
            third, fourth = result[2 * height : 3 * height], result[3 * height :]
            keep_ref[p, half] = jnp.where(even, third, fourth)
            send_ref[p, half] = jnp.where(even, fourth, third)


def route_kernel(groups, *refs):
    came, (keep_ref, send_ref, held) = refs[:groups], refs[groups:]
    f, c, _ = place()
    for p in range(groups):
        held[p] = came[p][...]
    for m in range(0, groups, 2):
        keep_ref[m // 2] = held[c ^ f ^ m]
        send_ref[m // 2] = held[c ^ f ^ m ^ 1]


def add_kernel(groups, *refs):
    keep_ref, came_ref, *rest = refs
    straight, outs = rest[: groups // 2 - 1], rest[groups // 2 - 1 :]
    for i in range(1, groups // 2):
        total = keep_ref[i].astype(F32) + came_ref[i].astype(F32)
        rows = total.shape[1]
        outs[i - 1][:, :rows] = total.astype(BF16)
        outs[i - 1][:, rows:] = straight[i - 1][...]


def merge_kernel(groups, keep_ref, came_ref, *outs):
    for p in range(groups):
        outs[p][...] = (keep_ref[p].astype(F32) + came_ref[p].astype(F32)).astype(BF16)


def direct_kernel(groups, *refs):
    came, outs, held = refs[:groups], refs[groups : 2 * groups], refs[2 * groups]
    f, c, _ = place()
    for p in range(groups):
        held[p] = came[p][...]
    for m in range(groups):
        outs[m][...] = held[c ^ f ^ m]


def finish_kernel(groups, *refs):
    keep_ref, came_ref, mine_ref, *rest = refs[:-2]
    bias_ref, out_ref = refs[-2:]
    far, odd = rest[: groups // 2 - 1], rest[groups // 2 - 1 :]
    f, _, _ = place()
    _, rows, wslice = mine_ref.shape
    for half in range(2):
        cols = slice(half * wslice, (half + 1) * wslice)
        bias = bias_ref[pl.ds(2 * f + half, 1), :]
        first = keep_ref[0, half].astype(F32) + came_ref[0, half].astype(F32)
        same = mine_ref[half].astype(F32)
        for ref in far:
            first += ref[half, : 2 * rows].astype(F32)
            same += ref[half, 2 * rows :].astype(F32)
        out_ref[: 2 * rows, cols] = (first + bias).astype(BF16)
        other = odd[0][half].astype(F32)
        for ref in odd[1:]:
            other += ref[half].astype(F32)
        for total, parity in ((same, f & 1), (other, 1 - (f & 1))):
            start = pl.multiple_of(2 * rows + parity * rows, rows)
            out_ref[pl.ds(start, rows), cols] = (total + bias).astype(BF16)


def on_device(tokens, dec_bias, enc_weight, enc_bias, dec_weight, block_ids, block_counts):
    tile_count = lax.axis_size("tok")
    groups = lax.axis_size("feat")
    tok_rows, width = tokens.shape
    wslice = width // tile_count
    feats = enc_weight.shape[1]
    ids = block_ids[:, 0, :]
    counts = block_counts[:, 0]
    bias_rows = dec_bias.astype(F32).reshape(tile_count, wslice)
    enc_bias_rows = enc_bias.astype(F32).reshape(feats // LANES, LANES)

    def swap(value, p):
        pairs = [(i, i ^ (2 * p)) for i in range(tile_count)]
        return lax.ppermute(value, "tok", pairs)

    def lift(value, m):
        return lax.ppermute(value, "feat", [(i, i ^ m) for i in range(groups)])

    cores = [(i, i ^ 1) for i in range(tile_count)]
    enc_other = lax.ppermute(enc_weight, "tok", cores)
    dec_other = lax.ppermute(dec_weight, "tok", cores)

    sent = pl.pallas_call(
        functools.partial(split_kernel, groups),
        out_shape=[jax.ShapeDtypeStruct((2, tok_rows, wslice), BF16)] * groups,
        in_specs=[spec(pl.ANY)] * 2,
        out_specs=[spec(VMEM)] * groups,
        scratch_shapes=[
            VMEM((tok_rows, width), BF16),
            VMEM((width,), BF16),
            pltpu.SemaphoreType.DMA((5,)),
        ],
        compiler_params=params(8),
        cost_estimate=cost(0, 4 * width * tok_rows),
        name="split",
    )(pin(tokens), pin(dec_bias))
    pieces = [sent[0]] + [swap(sent[p], p) for p in range(1, groups)]

    def columns(weight):
        return pl.pallas_call(
            functools.partial(columns_kernel, groups),
            out_shape=jax.ShapeDtypeStruct((groups, wslice, ACTIVE), BF16),
            in_specs=[spec(SMEM), spec(VMEM)],
            out_specs=spec(VMEM),
            compiler_params=params(8),
            cost_estimate=cost(0, 2 * wslice * (feats + groups * ACTIVE)),
            name="columns",
        )(ids, weight)

    own_cols = columns(enc_weight)
    oth_cols = columns(enc_other)
    flops = 4 * groups * tok_rows * wslice * ACTIVE
    part = []
    for low, high in ((0, groups // 2), (groups // 2, groups)):
        part = [
            pl.pallas_call(
                functools.partial(encode_kernel, groups, low),
                out_shape=jax.ShapeDtypeStruct((high, tok_rows, ACTIVE), BF16),
                in_specs=[spec(VMEM)] * (2 + len(part) + high - low),
                out_specs=spec(VMEM),
                compiler_params=params(8),
                cost_estimate=cost(flops // 2, 2 * groups * wslice * ACTIVE),
                name="encode",
            )(own_cols, oth_cols, *part, *pieces[low:high])
        ]
    part = part[0]
    parts = [part] + [swap(part, p) for p in range(1, groups)]

    dec_staged = pl.pallas_call(
        stage_kernel,
        out_shape=jax.ShapeDtypeStruct(dec_weight.shape, BF16),
        in_specs=[spec(pl.ANY)],
        out_specs=spec(VMEM),
        scratch_shapes=[pltpu.SemaphoreType.DMA((8,))],
        compiler_params=params(8),
        cost_estimate=cost(0, 4 * wslice * feats),
        name="stage",
    )(dec_other)
    half_rows = tok_rows // 2
    quarter_rows = tok_rows // 4
    piece = jax.ShapeDtypeStruct((2, half_rows, wslice), BF16)
    small = jax.ShapeDtypeStruct((2, quarter_rows, wslice), BF16)
    smalls = jax.ShapeDtypeStruct((groups, 2, quarter_rows, wslice), BF16)
    code_values, *outgoing = pl.pallas_call(
        functools.partial(decode_kernel, groups),
        out_shape=[jax.ShapeDtypeStruct((tok_rows, ACTIVE), BF16)]
        + [piece] * groups
        + [smalls] * 2,
        in_specs=[spec(SMEM)] * 2 + [spec(VMEM)] * (3 + groups),
        out_specs=[spec(VMEM)] * (3 + groups),
        compiler_params=params(8),
        cost_estimate=cost(flops, 4 * groups * wslice * ACTIVE),
        name="decode",
    )(ids, counts, enc_bias_rows, *parts, dec_weight, dec_staged)
    firsts, (own_sums, sent_sums) = outgoing[:groups], outgoing[groups:]

    swapped = lift(sent_sums, 1)
    came = [firsts[0]] + [swap(firsts[p], p) for p in range(1, groups)]
    merged = pl.pallas_call(
        functools.partial(merge_kernel, groups),
        out_shape=[small] * groups,
        in_specs=[spec(VMEM)] * 2,
        out_specs=[spec(VMEM)] * groups,
        compiler_params=params(8),
        cost_estimate=cost(0, 8 * groups * quarter_rows * wslice),
        name="merge",
    )(own_sums, swapped)
    came[0], *merged = lax.optimization_barrier((came[0], *merged))
    both = jax.ShapeDtypeStruct((groups // 2,) + piece.shape, BF16)
    keep, send = pl.pallas_call(
        functools.partial(route_kernel, groups),
        out_shape=[both] * 2,
        in_specs=[spec(VMEM)] * groups,
        out_specs=[spec(VMEM)] * 2,
        scratch_shapes=[VMEM((groups,) + piece.shape, BF16)],
        compiler_params=params(8),
        cost_estimate=cost(0, 8 * groups * half_rows * wslice),
        name="route",
    )(*came)
    near = lift(send, 1)
    merged = [merged[0]] + [swap(merged[p], p) for p in range(1, groups)]
    direct = pl.pallas_call(
        functools.partial(direct_kernel, groups),
        out_shape=[small] * groups,
        in_specs=[spec(VMEM)] * groups,
        out_specs=[spec(VMEM)] * groups,
        scratch_shapes=[VMEM((groups,) + small.shape, BF16)],
        compiler_params=params(8),
        cost_estimate=cost(0, 8 * groups * quarter_rows * wslice),
        name="direct",
    )(*merged)
    far = jax.ShapeDtypeStruct((2, half_rows + quarter_rows, wslice), BF16)
    sums = pl.pallas_call(
        functools.partial(add_kernel, groups),
        out_shape=[far] * (groups // 2 - 1),
        in_specs=[spec(VMEM)] * (1 + groups // 2),
        out_specs=[spec(VMEM)] * (groups // 2 - 1),
        compiler_params=params(8),
        cost_estimate=cost(groups * half_rows * wslice, 6 * groups * half_rows * wslice),
        name="add",
    )(keep, near, *direct[2::2])
    moved = [keep, near, direct[0]]
    moved += [lift(sums[m // 2 - 1], m) for m in range(2, groups, 2)]
    moved += [lift(direct[m], m) for m in range(1, groups, 2)]

    rebuilt = pl.pallas_call(
        functools.partial(finish_kernel, groups),
        out_shape=jax.ShapeDtypeStruct((tok_rows, 2 * wslice), BF16),
        in_specs=[spec(VMEM)] * (len(moved) + 1),
        out_specs=spec(VMEM),
        compiler_params=params(8),
        cost_estimate=cost(0, 4 * (groups + 1) * tok_rows * wslice),
        name="finish",
    )(*moved, bias_rows)
    return (code_values, rebuilt)


def solution(mesh):
    in_specs = (
        P("tok", None),
        P(),
        P("tok", "feat"),
        P("feat"),
        P("feat", "tok"),
        P(None, "feat", None),
        P(None, "feat"),
    )
    out_specs = (P("tok", "feat"), P("tok", "feat"))
    return jax.shard_map(
        on_device, mesh=mesh, in_specs=in_specs, out_specs=out_specs, check_vma=False
    )
```

```python
import functools

import jax
import jax.numpy as jnp
from jax import lax
from jax.experimental import pallas as pl
from jax.experimental.pallas import tpu as pltpu
from jax.sharding import PartitionSpec as P

BLOCK = 64
SLOTS = 4
LANES = 128
ACTIVE = SLOTS * BLOCK
VMEM = pltpu.VMEM
SMEM = pltpu.SMEM
HBM = pltpu.HBM
BF16 = jnp.bfloat16
F32 = jnp.float32


def spec(space):
    return pl.BlockSpec(memory_space=space)


def params(mib):
    return pltpu.CompilerParams(vmem_limit_bytes=mib << 20)


def cost(flops, nbytes):
    return pl.CostEstimate(flops=flops, bytes_accessed=nbytes, transcendentals=0)


def pin(value):
    return pltpu.with_memory_space_constraint(value, HBM)


def place():
    tok = lax.axis_index("tok")
    return lax.axis_index("feat"), tok >> 1, tok & 1


def split_kernel(groups, tok_ref, bias_ref, *refs):
    outs, (held, bias, sems) = refs[:groups], refs[groups:]
    _, c, k = place()
    wslice = outs[0].shape[2]
    parts = sems.shape[0] - 1
    height = held.shape[0] // parts
    copies = [pltpu.make_async_copy(bias_ref, bias, sems.at[parts])]
    for i in range(parts):
        some = pl.ds(i * height, height)
        copies.append(pltpu.make_async_copy(tok_ref.at[some, :], held.at[some, :], sems.at[i]))
    for copy in copies:
        copy.start()
    copies[0].wait()
    for i, copy in enumerate(copies[1:]):
        copy.wait()
        some = slice(i * height, (i + 1) * height)
        for p in range(groups):
            for half in range(2):
                u = ((c ^ p) << 1) + (k ^ half)
                cols = pl.ds(pl.multiple_of(u * wslice, wslice), wslice)
                value = held[some, cols].astype(F32) - bias[cols].astype(F32)[None, :]
                outs[p][half, some] = value.astype(BF16)


def pick_pair(first, second, odd_first, odd_second):
    low = lax.broadcasted_iota(jnp.int32, first.shape, 1) < BLOCK
    a = jnp.where(odd_first, pltpu.roll(first, BLOCK, 1), first)
    b = jnp.where(odd_second, second, pltpu.roll(second, BLOCK, 1))
    return jnp.where(low, a, b)


def columns_kernel(groups, ids_ref, w_ref, out_ref):
    _, c, k = place()
    low = lax.broadcasted_iota(jnp.int32, (w_ref.shape[0], LANES), 1) < BLOCK
    for p in range(groups):
        tile = ((c ^ p) << 1) + k
        for pair in range(SLOTS // 2):
            halves = []
            for slot in range(2):
                block = ids_ref[tile, 2 * pair + slot]
                start = pl.multiple_of((block >> 1) * LANES, LANES)
                turn = ((block & 1) ^ slot) * BLOCK
                halves.append(pltpu.roll(w_ref[:, pl.ds(start, LANES)], turn, 1))
            out_ref[p, :, pair * LANES : (pair + 1) * LANES] = jnp.where(low, *halves)


def stage_kernel(src, dst, sems):
    parts = sems.shape[0]
    height = src.shape[0] // parts
    copies = []
    for i in range(parts):
        some = pl.ds(i * height, height)
        copy = pltpu.make_async_copy(src.at[some, :], dst.at[some, :], sems.at[i])
        copy.start()
        copies.append(copy)
    for copy in copies:
        copy.wait()


def encode_kernel(groups, low, *refs):
    own_ref, oth_ref = refs[:2]
    done, pieces, out_ref = refs[2 : 2 + bool(low)], refs[2 + bool(low) : -1], refs[-1]
    for ref in done:
        out_ref[:low] = ref[...]
    for p, ref in enumerate(pieces, low):
        acc = jnp.dot(ref[0], own_ref[p], preferred_element_type=F32)
        acc += jnp.dot(ref[1], oth_ref[p], preferred_element_type=F32)
        out_ref[p] = acc.astype(BF16)


def decode_kernel(groups, *refs):
    ids_ref, counts_ref, bias_ref = refs[:3]
    parts = refs[3 : 3 + groups]
    own_ref, oth_ref, code_ref = refs[3 + groups : 6 + groups]
    firsts = refs[6 + groups : 6 + 2 * groups]
    keep_ref, send_ref = refs[6 + 2 * groups :]
    f, c, k = place()
    even = (f & 1) == 0
    lane = lax.broadcasted_iota(jnp.int32, (1, LANES), 1)
    for p in range(groups):
        tile = ((c ^ p) << 1) + k
        count = counts_ref[tile]
        code = []
        listed = []
        for pair in range(SLOTS // 2):
            cols = slice(pair * LANES, (pair + 1) * LANES)
            pre = parts[0][p, :, cols].astype(F32)
            for q in range(1, groups):
                pre += parts[q][p ^ q, :, cols].astype(F32)
            bias = []
            odds = []
            for slot in (2 * pair, 2 * pair + 1):
                block = ids_ref[tile, slot]
                listed.append(pl.ds(pl.multiple_of(block * BLOCK, BLOCK), BLOCK))
                bias.append(bias_ref[pl.ds(block >> 1, 1), :])
                odds.append((block & 1) == 1)
            row = pick_pair(bias[0], bias[1], *odds)
            live = (lane >= BLOCK).astype(jnp.int32) + 2 * pair < count
            value = jnp.where(live, jnp.maximum(pre + row, 0.0), 0.0).astype(BF16)
            code.append(value)
        code = jnp.concatenate(code, axis=1)
        if p == 0:
            code_ref[...] = code
        height = code.shape[0] // 4
        for half, ref in ((k, own_ref), (1 - k, oth_ref)):
            rows = jnp.concatenate([ref[some, :] for some in listed], axis=0)
            result = jnp.dot(code, rows, preferred_element_type=F32).astype(BF16)
            firsts[p][half] = result[: 2 * height]
            third, fourth = result[2 * height : 3 * height], result[3 * height :]
            keep_ref[p, half] = jnp.where(even, third, fourth)
            send_ref[p, half] = jnp.where(even, fourth, third)


def route_kernel(groups, *refs):
    came, (keep_ref, send_ref, held) = refs[:groups], refs[groups:]
    f, c, _ = place()
    for p in range(groups):
        held[p] = came[p][...]
    for m in range(0, groups, 2):
        keep_ref[m // 2] = held[c ^ f ^ m]
        send_ref[m // 2] = held[c ^ f ^ m ^ 1]


def add_kernel(groups, *refs):
    keep_ref, came_ref, *rest = refs
    straight, outs = rest[: groups // 2 - 1], rest[groups // 2 - 1 :]
    for i in range(1, groups // 2):
        total = keep_ref[i].astype(F32) + came_ref[i].astype(F32)
        rows = total.shape[1]
        outs[i - 1][:, :rows] = total.astype(BF16)
        outs[i - 1][:, rows:] = straight[i - 1][...]


def merge_kernel(groups, keep_ref, came_ref, *outs):
    for p in range(groups):
        outs[p][...] = (keep_ref[p].astype(F32) + came_ref[p].astype(F32)).astype(BF16)


def direct_kernel(groups, *refs):
    came, outs, held = refs[:groups], refs[groups : 2 * groups], refs[2 * groups]
    f, c, _ = place()
    for p in range(groups):
        held[p] = came[p][...]
    for m in range(groups):
        outs[m][...] = held[c ^ f ^ m]


def finish_kernel(groups, *refs):
    keep_ref, came_ref, mine_ref, *rest = refs[:-2]
    bias_ref, out_ref = refs[-2:]
    far, odd = rest[: groups // 2 - 1], rest[groups // 2 - 1 :]
    f, _, _ = place()
    _, rows, wslice = mine_ref.shape
    for half in range(2):
        cols = slice(half * wslice, (half + 1) * wslice)
        bias = bias_ref[pl.ds(2 * f + half, 1), :]
        first = keep_ref[0, half].astype(F32) + came_ref[0, half].astype(F32)
        same = mine_ref[half].astype(F32)
        for ref in far:
            first += ref[half, : 2 * rows].astype(F32)
            same += ref[half, 2 * rows :].astype(F32)
        out_ref[: 2 * rows, cols] = (first + bias).astype(BF16)
        other = odd[0][half].astype(F32)
        for ref in odd[1:]:
            other += ref[half].astype(F32)
        for total, parity in ((same, f & 1), (other, 1 - (f & 1))):
            start = pl.multiple_of(2 * rows + parity * rows, rows)
            out_ref[pl.ds(start, rows), cols] = (total + bias).astype(BF16)


def on_device(tokens, dec_bias, enc_weight, enc_bias, dec_weight, block_ids, block_counts):
    tile_count = lax.axis_size("tok")
    groups = lax.axis_size("feat")
    tok_rows, width = tokens.shape
    wslice = width // tile_count
    feats = enc_weight.shape[1]
    ids = block_ids[:, 0, :]
    counts = block_counts[:, 0]
    bias_rows = dec_bias.astype(F32).reshape(tile_count, wslice)
    enc_bias_rows = enc_bias.astype(F32).reshape(feats // LANES, LANES)

    def swap(value, p):
        pairs = [(i, i ^ (2 * p)) for i in range(tile_count)]
        return lax.ppermute(value, "tok", pairs)

    def lift(value, m):
        return lax.ppermute(value, "feat", [(i, i ^ m) for i in range(groups)])

    cores = [(i, i ^ 1) for i in range(tile_count)]
    enc_other = lax.ppermute(enc_weight, "tok", cores)
    dec_other = lax.ppermute(dec_weight, "tok", cores)

    sent = pl.pallas_call(
        functools.partial(split_kernel, groups),
        out_shape=[jax.ShapeDtypeStruct((2, tok_rows, wslice), BF16)] * groups,
        in_specs=[spec(pl.ANY)] * 2,
        out_specs=[spec(VMEM)] * groups,
        scratch_shapes=[
            VMEM((tok_rows, width), BF16),
            VMEM((width,), BF16),
            pltpu.SemaphoreType.DMA((5,)),
        ],
        compiler_params=params(8),
        cost_estimate=cost(0, 4 * width * tok_rows),
        name="split",
    )(pin(tokens), pin(dec_bias))
    pieces = [sent[0]] + [swap(sent[p], p) for p in range(1, groups)]

    def columns(weight):
        return pl.pallas_call(
            functools.partial(columns_kernel, groups),
            out_shape=jax.ShapeDtypeStruct((groups, wslice, ACTIVE), BF16),
            in_specs=[spec(SMEM), spec(VMEM)],
            out_specs=spec(VMEM),
            compiler_params=params(8),
            cost_estimate=cost(0, 2 * wslice * (feats + groups * ACTIVE)),
            name="columns",
        )(ids, weight)

    own_cols = columns(enc_weight)
    oth_cols = columns(enc_other)
    flops = 4 * groups * tok_rows * wslice * ACTIVE
    part = []
    for low, high in ((0, groups // 2), (groups // 2, groups)):
        part = [
            pl.pallas_call(
                functools.partial(encode_kernel, groups, low),
                out_shape=jax.ShapeDtypeStruct((high, tok_rows, ACTIVE), BF16),
                in_specs=[spec(VMEM)] * (2 + len(part) + high - low),
                out_specs=spec(VMEM),
                compiler_params=params(8),
                cost_estimate=cost(flops // 2, 2 * groups * wslice * ACTIVE),
                name="encode",
            )(own_cols, oth_cols, *part, *pieces[low:high])
        ]
    part = part[0]
    parts = [part] + [swap(part, p) for p in range(1, groups)]

    dec_staged = pl.pallas_call(
        stage_kernel,
        out_shape=jax.ShapeDtypeStruct(dec_weight.shape, BF16),
        in_specs=[spec(pl.ANY)],
        out_specs=spec(VMEM),
        scratch_shapes=[pltpu.SemaphoreType.DMA((8,))],
        compiler_params=params(8),
        cost_estimate=cost(0, 4 * wslice * feats),
        name="stage",
    )(dec_other)
    half_rows = tok_rows // 2
    quarter_rows = tok_rows // 4
    piece = jax.ShapeDtypeStruct((2, half_rows, wslice), BF16)
    small = jax.ShapeDtypeStruct((2, quarter_rows, wslice), BF16)
    smalls = jax.ShapeDtypeStruct((groups, 2, quarter_rows, wslice), BF16)
    code_values, *outgoing = pl.pallas_call(
        functools.partial(decode_kernel, groups),
        out_shape=[jax.ShapeDtypeStruct((tok_rows, ACTIVE), BF16)]
        + [piece] * groups
        + [smalls] * 2,
        in_specs=[spec(SMEM)] * 2 + [spec(VMEM)] * (3 + groups),
        out_specs=[spec(VMEM)] * (3 + groups),
        compiler_params=params(8),
        cost_estimate=cost(flops, 4 * groups * wslice * ACTIVE),
        name="decode",
    )(ids, counts, enc_bias_rows, *parts, dec_weight, dec_staged)
    firsts, (own_sums, sent_sums) = outgoing[:groups], outgoing[groups:]

    swapped = lift(sent_sums, 1)
    came = [firsts[0]] + [swap(firsts[p], p) for p in range(1, groups)]
    merged = pl.pallas_call(
        functools.partial(merge_kernel, groups),
        out_shape=[small] * groups,
        in_specs=[spec(VMEM)] * 2,
        out_specs=[spec(VMEM)] * groups,
        compiler_params=params(8),
        cost_estimate=cost(0, 8 * groups * quarter_rows * wslice),
        name="merge",
    )(own_sums, swapped)
    came[0], *merged = lax.optimization_barrier((came[0], *merged))
    both = jax.ShapeDtypeStruct((groups // 2,) + piece.shape, BF16)
    keep, send = pl.pallas_call(
        functools.partial(route_kernel, groups),
        out_shape=[both] * 2,
        in_specs=[spec(VMEM)] * groups,
        out_specs=[spec(VMEM)] * 2,
        scratch_shapes=[VMEM((groups,) + piece.shape, BF16)],
        compiler_params=params(8),
        cost_estimate=cost(0, 8 * groups * half_rows * wslice),
        name="route",
    )(*came)
    near = lift(send, 1)
    merged = [merged[0]] + [swap(merged[p], p) for p in range(1, groups)]
    direct = pl.pallas_call(
        functools.partial(direct_kernel, groups),
        out_shape=[small] * groups,
        in_specs=[spec(VMEM)] * groups,
        out_specs=[spec(VMEM)] * groups,
        scratch_shapes=[VMEM((groups,) + small.shape, BF16)],
        compiler_params=params(8),
        cost_estimate=cost(0, 8 * groups * quarter_rows * wslice),
        name="direct",
    )(*merged)
    far = jax.ShapeDtypeStruct((2, half_rows + quarter_rows, wslice), BF16)
    sums = pl.pallas_call(
        functools.partial(add_kernel, groups),
        out_shape=[far] * (groups // 2 - 1),
        in_specs=[spec(VMEM)] * (1 + groups // 2),
        out_specs=[spec(VMEM)] * (groups // 2 - 1),
        compiler_params=params(8),
        cost_estimate=cost(groups * half_rows * wslice, 6 * groups * half_rows * wslice),
        name="add",
    )(keep, near, *direct[2::2])
    moved = [keep, near, direct[0]]
    moved += [lift(sums[m // 2 - 1], m) for m in range(2, groups, 2)]
    moved += [lift(direct[m], m) for m in range(1, groups, 2)]

    rebuilt = pl.pallas_call(
        functools.partial(finish_kernel, groups),
        out_shape=jax.ShapeDtypeStruct((tok_rows, 2 * wslice), BF16),
        in_specs=[spec(VMEM)] * (len(moved) + 1),
        out_specs=spec(VMEM),
        compiler_params=params(8),
        cost_estimate=cost(0, 4 * (groups + 1) * tok_rows * wslice),
        name="finish",
    )(*moved, bias_rows)
    return (code_values, rebuilt)


def solution(mesh):
    in_specs = (
        P("tok", None),
        P(),
        P("tok", "feat"),
        P("feat"),
        P("feat", "tok"),
        P(None, "feat", None),
        P(None, "feat"),
    )
    out_specs = (P("tok", "feat"), P("tok", "feat"))
    return jax.shard_map(
        on_device, mesh=mesh, in_specs=in_specs, out_specs=out_specs, check_vma=False
    )
```
